512 devices in a mesh: expert: 16 (over y, core), dp: 32 (over z, x).
Axes of the slice: x: 4, y: 8, z: 8, core: 2. Of those that a mesh axis runs over, the one named last changes fastest.
Arguments:
- tokens: bfloat16 [768, 3072], P('dp'), may hold values from -6 to 6
- routes: int32 [768, 2], replicated, may hold values from 0 to 7, all different within a row; in each aligned block of 24 rows (0 to 23, 24 to 47, ...) at most 12 rows name the same one
- w_router: bfloat16 [3072, 8], replicated, may hold values from -0.109375 to 0.109375
- norm_gain: float32 [3072], replicated, may hold values from 0.25 to 1.75
- w_gate: bfloat16 [16, 3072, 4096], P('expert', None, 'dp'), may hold values from -0.109375 to 0.109375
- w_up: bfloat16 [16, 3072, 4096], P('expert', None, 'dp'), may hold values from -0.109375 to 0.109375
- w_down: bfloat16 [16, 4096, 3072], P('expert', 'dp'), may hold values from -0.09375 to 0.09375
- final_gain: float32 [3072], replicated, may hold values from 0.25 to 1.75
- head_weights: bfloat16 [4, 3072, 3072], P(None, 'dp', 'expert'), may hold values from -0.109375 to 0.109375
- vocab_proj: bfloat16 [3072, 16384], P('dp', 'expert'), may hold values from -0.21650635 to 0.21650635
Outputs:
- head_losses: float32 [4], replicated
- head_grads: float32 [4, 3072, 3072], P(None, 'dp', 'expert')
The draws below stay inside these ranges and needn't reach their ends.
Inputs may be any that keep to these rules, and one draw needn't show every extreme that they name: `routes`: in each aligned block of 24 rows (one token block) no expert is named by more than 12 rows, a bound that some block reaches; the two entries of a row differ.
All inputs are finite; a program needn't handle non-finite values.
Results may differ from the reference program's by a relative error of at most 0.04.
Values may be sent and summed in bfloat16 or wider, within the bound.
A program may use at most 64 MiB of HBM per device.

```python
import math
import jax
import jax.numpy as jnp
import numpy as np
from jax import lax

D = 3072
FF = 8192
VOCAB = 16384
HEADS = 4
TOK_DEV = 24
EXPERTS = 8
CAP = 12
TOKENS = 768
N_DP = 32


def draw_vocab_proj(key, part):
    column = jnp.arange(VOCAB, dtype=jnp.float32) / jnp.float32(VOCAB - 1)
    rise = jnp.exp(column * jnp.log(jnp.float32(1.6)))
    entries = jax.random.normal(key, (D, VOCAB), jnp.float32)
    spread = 1.2 / jnp.sqrt(jnp.float32(D))
    limit = 12.0 / jnp.sqrt(jnp.float32(D))
    return jnp.clip(entries * rise[None, :] * spread, -limit, limit).astype(jnp.bfloat16)


def steps_of(key, shape, shards, smallest, high):
    gain, own = 1.0, jax.random.fold_in(key, 6)
    for dim, blocks in shards:
        heights = jnp.exp(jax.random.uniform(jax.random.fold_in(own, dim), (blocks,), jnp.float32, smallest / len(shards), high / len(shards)))
        gain = gain * jnp.repeat(heights, shape[dim] // blocks).reshape([-1 if axis == dim else 1 for axis in range(len(shape))])
    return gain


def routed_block(rng, own, number, rows, amount, top, reach, lean):
    ranking = jax.random.permutation(rng, amount)
    heavy_load, ordinary = shares(amount, rows * top, reach, lean, True), shares(amount, rows * top, reach, lean, False)
    places = jnp.arange(amount)

    def named(tallies, offset_by):
        used = int((tallies > 0).sum())
        fixed = max(1, used // 4)
        shifted = fixed + (places - fixed + offset_by * (used - fixed)) % max(1, amount - fixed)
        return jnp.zeros((amount,), jnp.int32).at[ranking[jnp.where(places < fixed, places, shifted)]].set(jnp.asarray(tallies, jnp.int32))

    tallies = jnp.where(number % 4 == 0, named(heavy_load, number // 4), named(ordinary, number - number // 4 - 1))
    mixed = jax.random.permutation(jax.random.fold_in(own, 3), amount)
    giver, receiver = mixed[0:amount // 2 * 2:2], mixed[1:amount // 2 * 2:2]
    room = jnp.minimum(tallies[giver] - 1, reach - tallies[receiver]) // 2
    room = jnp.where((giver == ranking[0]) | (receiver == ranking[0]) | (tallies[receiver] == 0), 0, jnp.maximum(room, 0))
    shifted = jax.random.randint(jax.random.fold_in(own, 4), (amount // 2,), 0, 1 << 20) % (room + 1)
    tallies = tallies.at[giver].add(-shifted).at[receiver].add(shifted)
    labels = jnp.searchsorted(jnp.cumsum(tallies), jnp.arange(rows * top), side="right").astype(jnp.int32)
    grid = labels.reshape(top, rows).T
    grid = grid[jax.random.permutation(jax.random.fold_in(own, 1), rows)]
    offset_by = jax.random.randint(jax.random.fold_in(own, 2), (rows, 1), 0, top)
    return jnp.take_along_axis(grid, (jnp.arange(top)[None, :] + offset_by) % top, axis=1)


def shares(amount, total, reach, lean, full):
    weights = [(1 << 20) // math.isqrt(rank ** lean) + 1 for rank in range(1, amount + 1)]
    largest = reach if full else min(reach, max(-(-total // amount), total * weights[0] // sum(weights)))
    least = 1 if total - largest >= amount - 1 else 0
    holding, rest = [largest] + [least] * (amount - 1), total - largest - least * (amount - 1)
    while rest > 0:
        movable = [i for i in range(1, amount) if holding[i] < largest] or [i for i in range(1, amount) if holding[i] < reach]
        mass, budget = sum([weights[i] for i in movable]), rest
        for i in movable:
            extra = min(reach - holding[i], max(1, budget * weights[i] // mass), rest)
            holding[i] = holding[i] + extra
            rest = rest - extra
    return np.array(holding)


def bell_draw(rng, extent, scale, most, cuts=(), kind=jnp.bfloat16):
    gain = steps_of(rng, extent, cuts, -0.22, 0.18) if cuts else 1.0
    values = jax.random.normal(rng, extent, jnp.float32) * scale * gain
    return jnp.minimum(jnp.maximum(values, -most), most).astype(kind)


def setup_inputs(seed: int = 0) -> dict:
    seeds = jax.random.split(jax.random.key(seed), 11)
    tokens = bell_draw(seeds[0], (TOKENS, D), 1.0, 6.0, ((0, 32),))
    routes_keys = jax.random.split(jax.random.fold_in(seeds[1], 1), TOKENS // TOK_DEV)
    routes_turns = jax.random.permutation(jax.random.fold_in(seeds[1], 3), TOKENS // TOK_DEV)
    routes = jax.vmap(lambda own, number: routed_block(jax.random.fold_in(seeds[1], 2), own, number, TOK_DEV, EXPERTS, 2, CAP, 2))(routes_keys, routes_turns).reshape((TOKENS, 2))
    w_router = bell_draw(seeds[2], (D, EXPERTS), D ** -0.5, 0.109375)
    norm_gain = jnp.clip(1.0 + 0.15 * jax.random.normal(seeds[3], (D,), jnp.float32), 0.25, 1.75)
    w_gate = bell_draw(seeds[4], (2 * EXPERTS, D, FF // 2), D ** -0.5, 0.109375, ((0, 16), (2, 32)))
    w_up = bell_draw(seeds[5], (2 * EXPERTS, D, FF // 2), D ** -0.5, 0.109375, ((0, 16), (2, 32)))
    w_down = bell_draw(seeds[6], (2 * EXPERTS, FF // 2, D), (FF // 2) ** -0.5, 0.09375, ((0, 16), (1, 32)))
    final_gain = jnp.clip(1.0 + 0.15 * jax.random.normal(seeds[7], (D,), jnp.float32), 0.25, 1.75)
    head_weights = bell_draw(seeds[8], (HEADS, D, D), D ** -0.5, 0.109375, ((1, 32), (2, 16)))
    vocab_proj = draw_vocab_proj(jax.random.fold_in(seeds[10], 71), 0)
    return {"tokens": tokens, "routes": routes, "w_router": w_router, "norm_gain": norm_gain, "w_gate": w_gate, "w_up": w_up, "w_down": w_down, "final_gain": final_gain, "head_weights": head_weights, "vocab_proj": vocab_proj}


epsilon = 1e-05

def rms_scale(values, scale_gain):
    mean_square = lax.optimization_barrier(jnp.mean(values * values, axis=-1, keepdims=True))
    return values * lax.rsqrt(mean_square + epsilon) * scale_gain

def slot_tables(block_routes, experts, capacity):
    count_rows = block_routes.shape[0]
    flat_routes = block_routes.reshape(-1)
    expert_hot = (flat_routes[:, None] == jnp.arange(experts, dtype=jnp.int32)[None, :]).astype(jnp.int32)
    earlier = jnp.cumsum(expert_hot, axis=0) - expert_hot
    slot_number = lax.optimization_barrier(jnp.sum(earlier * expert_hot, axis=1))
    slot_hot = (slot_number[:, None] == jnp.arange(capacity, dtype=jnp.int32)[None, :]).astype(jnp.float32)
    return (expert_hot.astype(jnp.float32).reshape(count_rows, 2, experts), slot_hot.reshape(count_rows, 2, capacity))

def reference(tokens, routes, w_router, norm_gain, w_gate, w_up, w_down, final_gain, head_weights, vocab_proj):
    highest = lax.Precision.HIGHEST
    experts = w_router.shape[1]
    tokens_f32 = tokens.astype(jnp.float32)
    normed = rms_scale(tokens_f32, norm_gain).astype(jnp.bfloat16)
    router = jnp.dot(normed, w_router, preferred_element_type=jnp.float32)
    blocked = routes.reshape(N_DP, TOK_DEV, 2)
    expert_hot, slot_hot = jax.vmap(lambda block_routes: slot_tables(block_routes, experts, CAP))(blocked)
    router_blocks = router.reshape(N_DP, TOK_DEV, experts)
    chosen = lax.optimization_barrier(jnp.sum(router_blocks[:, :, None, :] * expert_hot, axis=-1))
    first = jax.nn.sigmoid(chosen[..., 0] - chosen[..., 1])
    gates = jnp.stack([first, 1.0 - first], axis=-1)
    select = jnp.einsum('btje,btjs->best', expert_hot, slot_hot, precision=highest)
    weighted = jnp.einsum('btje,btjs,btj->best', expert_hot, slot_hot, gates, precision=highest)
    blocks_f32 = normed.reshape(N_DP, TOK_DEV, D).astype(jnp.float32)
    inputs = jnp.einsum('best,btd->ebsd', select, blocks_f32, precision=highest).astype(jnp.bfloat16)
    group_width = FF // 2 // N_DP
    owners = jnp.arange(2 * experts, dtype=jnp.int32) // 2

    def half_output(packed):
        gate_half, up_half, down_half, owner = packed
        rows = lax.dynamic_index_in_dim(inputs, owner, 0, keepdims=False).reshape(N_DP * CAP, D)
        gate_pre = jnp.dot(rows, gate_half, preferred_element_type=jnp.float32)
        up_pre = jnp.dot(rows, up_half, preferred_element_type=jnp.float32)
        hidden = (jax.nn.silu(gate_pre) * up_pre).astype(jnp.bfloat16)
        grouped = hidden.reshape(N_DP * CAP, N_DP, group_width).astype(jnp.float32)
        down_grouped = down_half.reshape(N_DP, group_width, D).astype(jnp.float32)
        parts = jnp.einsum('rgf,gfo->gro', grouped, down_grouped, precision=highest)
        rounded = lax.optimization_barrier(parts.astype(jnp.bfloat16))
        return lax.optimization_barrier(jnp.sum(rounded.astype(jnp.float32), axis=0))
    outputs = lax.map(half_output, (w_gate, w_up, w_down, owners))
    outputs = outputs.reshape(2 * experts, N_DP, CAP, D)
    half_weights = weighted[:, owners]
    mixture = jnp.einsum('bqst,qbsd->btd', half_weights, outputs, precision=highest).reshape(TOKENS, D)
    final = rms_scale(tokens_f32 + mixture, final_gain).astype(jnp.bfloat16)
    teacher = jnp.dot(final, vocab_proj, preferred_element_type=jnp.float32)
    teacher_logp = teacher - jnp.log(lax.optimization_barrier(jnp.sum(jnp.exp(teacher), axis=-1)))[:, None]
    positions = jnp.arange(TOKENS, dtype=jnp.int32)
    losses = []
    grads = []
    for head_index in range(HEADS):
        ahead = head_index + 1
        preact = jnp.dot(final, head_weights[head_index], preferred_element_type=jnp.float32)
        student_in = (final.astype(jnp.float32) + jax.nn.silu(preact)).astype(jnp.bfloat16)
        student = jnp.dot(student_in, vocab_proj, preferred_element_type=jnp.float32)
        student_logp = student - jnp.log(lax.optimization_barrier(jnp.sum(jnp.exp(student), axis=-1)))[:, None]
        targets = jnp.concatenate([teacher_logp[ahead:], jnp.zeros((ahead, VOCAB), jnp.float32)], axis=0)
        row_weight = (positions + ahead < TOKENS).astype(jnp.float32) / jnp.float32(TOKENS - ahead)
        probs = jnp.exp(targets)
        divergence = lax.optimization_barrier(jnp.sum(probs * (targets - student_logp), axis=-1))
        losses.append(jnp.sum(row_weight * divergence))
        slopes = (row_weight[:, None] * (jnp.exp(student_logp) - probs)).astype(jnp.bfloat16)
        back = jnp.dot(slopes, vocab_proj.T, preferred_element_type=jnp.float32)
        sigma = jax.nn.sigmoid(preact)
        pre_grad = (back * sigma * (1.0 + preact * (1.0 - sigma))).astype(jnp.bfloat16)
        grads.append(jnp.dot(final.T, pre_grad, preferred_element_type=jnp.float32))
    return (jnp.stack(losses), jnp.stack(grads))
```

```python
import jax
import jax.numpy as jnp
from jax import lax
from jax.experimental import pallas as pl
from jax.experimental.pallas import tpu as pltpu
from jax.sharding import PartitionSpec as P

MESH = pl.DeviceIdType.MESH
F32, BF16 = jnp.float32, jnp.bfloat16
HIGHEST = lax.Precision.HIGHEST
EPS = 1e-05
NX = 4
TOK, CAP, SLOT = 24, 12, 16
N_COPIES = 190


def dot(a, b, dims=((1,), (0,)), precision=None):
    return lax.dot_general(a, b, (dims, ((), ())), precision=precision, preferred_element_type=F32)


def iota(shape, axis):
    return lax.broadcasted_iota(jnp.int32, shape, axis)


def one_hot(rows, cols, group, pitch):
    row = iota((rows, cols), 0)
    target = row
    for start in range(group, rows, group):
        target = target + jnp.where(row >= start, pitch - group, 0)
    return (target == iota((rows, cols), 1)).astype(BF16)


def spread(rows, cols, group, pitch):
    col = iota((rows, cols), 1)
    target = col
    for start in range(group, cols, group):
        target = target + jnp.where(col >= start, pitch - group, 0)
    return (target == iota((rows, cols), 0)).astype(BF16)


class Ring:
    def __init__(self, copy, n, me, plus, minus):
        self.copy, self.n, self.me, self.plus, self.minus = copy, n, me, plus, minus

    def at(self, offset):
        return lax.rem(self.me + (offset + self.n), self.n)


def body(
    nz, ny, tok_ref, routes_ref, wr_ref, ng_ref, fg_ref, hw_ref, wg_hbm, wu_hbm, wd_hbm, voc_hbm, loss_ref, out_ref,
    w_gu, wd, vg, hx, hl, hg, nbs, ax, ag, po, ps, pr, dl, rl, dr, rr, xs, xr, yg, sq, fp, f96, fw, fn, gfac, sg,
    ls, tl, sums, lsum, sl, bo, bs, br, el, erl, er, err, xs2, xr2, gg, osd, ord_, oown, r1, r2, q1, q2, q3,
    ss, rs, lsem,
):
    dp, ex = lax.axis_index("dp"), lax.axis_index("expert")
    z, x = lax.div(dp, NX), lax.rem(dp, NX)
    y, c = lax.div(ex, 2), lax.rem(ex, 2)
    oc = 1 - c
    d_model = tok_ref.shape[1]
    half = d_model // 2
    vcols = vg.shape[2]
    kcols = d_model // ny
    zrows = d_model // nz
    grp = NX * TOK
    hrow = grp // 2

    def dev(z_=None, x_=None, y_=None, c_=None):
        z_, x_ = (z if z_ is None else z_), (x if x_ is None else x_)
        y_, c_ = (y if y_ is None else y_), (c if c_ is None else c_)
        return {"dp": z_ * NX + x_, "expert": y_ * 2 + c_}

    def xo(d):
        return lax.rem(x + d, NX)

    def zo(d):
        return lax.rem(z + (d + nz), nz)

    def yo(d):
        return lax.rem(y + (d + ny), ny)

    partner = dev(c_=oc)
    sent = []

    def copy(src, dst, device):
        i = len(sent)
        cp = pltpu.make_async_remote_copy(
            src_ref=src, dst_ref=dst, send_sem=ss.at[i], recv_sem=rs.at[i], device_id=device, device_id_type=MESH
        )
        cp.start()
        sent.append(cp)
        return cp

    locals_ = []

    def local(src, dst):
        cp = pltpu.make_async_copy(src, dst, lsem.at[len(locals_)])
        cp.start()
        locals_.append(cp)
        return cp

    def arrive(copies):
        for cp in copies:
            cp.wait_recv()

    quarter = lambda x_: pl.ds(pl.multiple_of(x_ * vcols, 128), vcols)
    hcols = lambda c_: pl.ds(pl.multiple_of(c_ * half, 128), half)
    in_w = [
        local(wg_hbm, w_gu.at[:, 0:128]),
        local(wu_hbm, w_gu.at[:, 128:256]),
        local(wd_hbm.at[:, hcols(c)], wd.at[0]),
        local(wd_hbm.at[:, hcols(oc)], wd.at[1]),
    ]
    vrow = 96
    vslot = lambda x_: pl.ds(pl.multiple_of(x_ * vrow, 16), vrow)
    in_v = local(voc_hbm.at[:, quarter(x)], vg.at[z, vslot(x), :])

    barrier = pltpu.get_barrier_semaphore()
    line_z = [dev(z_=zo(d)) for d in range(1, nz)]
    line_y = [dev(y_=yo(d)) for d in range(1, ny)]
    near = [(xo(d), c_) for d in range(1, NX) for c_ in (c, oc)] + [(x, oc)]
    plane = [dev(x_=a, c_=b) for a, b in near]
    peers = line_z + line_y + plane
    for peer in peers:
        pl.semaphore_signal(barrier, inc=1, device_id=peer, device_id_type=MESH)

    tok = tok_ref[...].astype(F32)
    mean_square = jnp.sum(tok * tok, axis=-1, keepdims=True) * (1.0 / d_model)
    normed = (tok * lax.rsqrt(mean_square + EPS) * ng_ref[...]).astype(BF16)
    nbs[0] = normed[:, :half]
    nbs[1] = normed[:, half:]
    router = dot(normed, wr_ref[...], ((1,), (1,)))
    own_routes = routes_ref[pl.ds(pl.multiple_of(dp * TOK, 8), TOK), :]
    r0, r1_ = own_routes[:, 0:1], own_routes[:, 1:2]
    n_exp = router.shape[1]
    lane_e = iota((TOK, n_exp), 1)
    hot0, hot1 = (r0 == lane_e).astype(F32), (r1_ == lane_e).astype(F32)
    lower = (iota((TOK, TOK), 1) < iota((TOK, TOK), 0)).astype(BF16)
    earlier = dot(lower, (hot0 + hot1).astype(BF16))
    place0 = r0.astype(F32) * SLOT + jnp.sum(hot0 * earlier, axis=1, keepdims=True)
    place1 = r1_.astype(F32) * SLOT + jnp.sum(hot1 * earlier, axis=1, keepdims=True)
    first = jax.nn.sigmoid(jnp.sum(router * (hot0 - hot1), axis=1, keepdims=True))
    lane_f = iota((TOK, n_exp * SLOT), 1).astype(F32)
    weigh = first * (place0 == lane_f).astype(F32) + (1.0 - first) * (place1 == lane_f).astype(F32)
    weigh_hi = weigh.astype(BF16)
    weigh_lo = (weigh - weigh_hi.astype(F32)).astype(BF16)
    own_slot = (iota((TOK, SLOT), 1) + y * SLOT).astype(F32)
    select = ((place0 == own_slot).astype(F32) + (place1 == own_slot).astype(F32)).astype(BF16)
    ax[x] = dot(select, nbs[c], ((0,), (0,))).astype(BF16)

    pl.semaphore_wait(barrier, len(peers))

    def gather_ring(n, off, plus, minus, at, on_arrival):
        on_arrival(off(0))
        arrived = None
        for s in range(1, n // 2 + 1):
            a = copy(at(off(-(s - 1))), at(off(-(s - 1))), plus)
            b = copy(at(off(s - 1)), at(off(s - 1)), minus) if s < n // 2 else None
            yield
            a.wait_recv()
            on_arrival(off(-s))
            if b is not None:
                b.wait_recv()
                on_arrival(off(s))
        yield

    def run(gen):
        for _ in gen:
            pass

    nothing = lambda i: None

    def background():
        vx = [copy(voc_hbm.at[:, quarter(xo(d))], vg.at[z, vslot(x), :], dev(x_=xo(d))) for d in range(1, NX)]
        rows = lambda c_: pl.ds(pl.multiple_of(c_ * hrow, 16), hrow)
        ex_h = copy(hw_ref.at[:, rows(oc), :], hx, partner)
        yield
        ex_h.wait_recv()
        for k in range(NX):
            mine, theirs = hw_ref[k, rows(c), :], hx[k]
            left = jnp.where(c == 0, mine, theirs)
            right = jnp.where(c == 0, theirs, mine)
            hl[k] = jnp.concatenate([left, right], axis=1)
        hxc = [copy(hl.at[xo(d)], hg.at[z, x, c], dev(x_=xo(d))) for d in range(1, NX)]
        hg[z, x, c] = hl[x]
        yield
        arrive(hxc)
        forwards = []

        def forward(i):
            forwards.append(copy(hg.at[i, :, c], hg.at[i, :, c], partner))

        yield from gather_ring(nz, zo, dev(z_=zo(1)), dev(z_=zo(-1)), lambda i: hg.at[i, :, c], forward)
        arrive(forwards)
        yield "heads"
        arrive(vx)
        in_v.wait()
        yield from gather_ring(nz, zo, dev(z_=zo(1)), dev(z_=zo(-1)), lambda i: vg.at[i], nothing)

    bg = background()

    def step(n=1):
        for _ in range(n):
            next(bg, None)

    step()
    arrive([copy(ax.at[x], ax.at[x], dev(x_=xo(d))) for d in range(1, NX)])
    pick = one_hot(NX * CAP, NX * SLOT, CAP, SLOT)
    ag[c, z] = dot(pick, ax[...].reshape(NX * SLOT, half)).astype(BF16)
    step()
    fwd = []

    def forward_a(i):
        fwd.append(copy(ag.at[c, i], ag.at[c, i], partner))

    run(gather_ring(nz, zo, dev(z_=zo(1)), dev(z_=zo(-1)), lambda i: ag.at[c, i], forward_a))
    step()
    arrive(fwd)
    for cp in in_w:
        cp.wait()

    n_rows = nz * NX * CAP
    pre = dot(ag[0].reshape(n_rows, half), w_gu[:half, :]) + dot(ag[1].reshape(n_rows, half), w_gu[half:, :])
    gate, up = pre[:, :128], pre[:, 128:]
    hidden = (jax.nn.silu(gate) * up).astype(BF16)
    ps[...] = dot(hidden, wd[1]).astype(BF16).reshape(ps.shape)
    order = [4, 3, -3, 2, -2, 1, -1, 0]
    got = {}
    for o in order:
        got[o] = copy(ps.at[zo(o)], pr.at[zo(o)], partner)
    po[...] = dot(hidden, wd[0]).reshape(po.shape)
    step()

    def scatter_ring(n, off, plus, minus, own, got, left, in_left, right, in_right, between):
        h = n // 2
        a = b = None
        seen = set()

        def term(o):
            o = -h if o == h else o
            key = h if o == -h else o
            if key not in seen:
                got[key].wait_recv()
                seen.add(key)
            return own(off(o))

        for s in range(1, h + 1):
            value = term(-(h + 1 - s))
            if a is not None:
                a.wait_recv()
                value = value + in_left[s - 2].astype(F32)
            left[s - 1] = value.astype(BF16)
            a = copy(left.at[s - 1], in_left.at[s - 1], minus)
            if s < h:
                value = term(h - s)
                if b is not None:
                    b.wait_recv()
                    value = value + in_right[s - 2].astype(F32)
                right[s - 1] = value.astype(BF16)
                b = copy(right.at[s - 1], in_right.at[s - 1], plus)
            between()
        value = term(0)
        b.wait_recv()
        value = value + in_right[h - 2].astype(F32)
        a.wait_recv()
        return value + in_left[h - 1].astype(F32)

    total = scatter_ring(
        nz, zo, dev(z_=zo(1)), dev(z_=zo(-1)), lambda i: po[i] + pr[i].astype(F32), got, dl, rl, dr, rr, lambda: None
    )
    step()
    place = spread(NX * SLOT, NX * CAP, CAP, SLOT)
    xs[...] = dot(place, total.astype(BF16)).astype(BF16).reshape(xs.shape)
    arrive([copy(xs.at[xo(d)], xr.at[x], dev(x_=xo(d))) for d in range(1, NX)])
    rows = xs[x].astype(F32)
    for d in range(1, NX):
        rows = rows + xr[xo(d)].astype(F32)
    yg[y] = rows.astype(BF16)

    ycp = [copy(yg.at[y], yg.at[y], dev(y_=yo(d))) for d in range(1, ny)]
    step()
    arrive(ycp)
    outs = yg[...].reshape(ny * SLOT, half)
    mixed = tok_ref[:, hcols(c)].astype(F32) + dot(weigh_hi, outs) + dot(weigh_lo, outs)
    square = jnp.sum(mixed * mixed, axis=1, keepdims=True)
    sq[0] = jnp.broadcast_to(square, (TOK, 128))
    scp = copy(sq.at[0], sq.at[1], partner)
    scp.wait_recv()
    mean_square = (square + sq[1][:, 0:1]) * (1.0 / d_model)
    fin = (mixed * lax.rsqrt(mean_square + EPS) * fg_ref[:, hcols(c)]).astype(BF16)
    fp[c, x] = dot(spread(32, TOK, TOK, TOK), fin).astype(BF16)
    fcp = [copy(fp.at[c, x], fp.at[c, x], dev(x_=xo(d))) for d in range(1, NX)]
    fwd = [copy(fp.at[c, x], fp.at[c, x], partner)]
    for d, cp in zip(range(1, NX), fcp):
        cp.wait_recv()
        src = xo(NX - d)
        fwd.append(copy(fp.at[c, src], fp.at[c, src], partner))
    step()
    arrive(fwd)
    pick = one_hot(grp, NX * 32, TOK, 32)
    for h in range(2):
        f96[:, h * half : (h + 1) * half] = dot(pick, fp[h].reshape(NX * 32, half)).astype(BF16)

    hrows = pl.ds(pl.multiple_of(c * hrow, 16), hrow)

    def window(z_):
        start = jnp.minimum(lax.div((z_ * NX + x) * vrow, 128) * 128, d_model - 256)
        return pl.ds(pl.multiple_of(start, 128), 256)

    tcp = [copy(f96.at[hrows, window(zo(d))], fw.at[z], dev(z_=zo(d))) for d in range(1, nz)]
    fw[z] = f96[hrows, window(z)]
    ncp = copy(f96.at[0:16, :], fn, dev(z_=zo(-1)))

    while next(bg, "heads") != "heads":
        pass
    ycols = lambda y_: pl.ds(pl.multiple_of(y_ * kcols, 128), kcols)
    preact = dot(f96[hrows, :], hg[...].reshape(d_model, kcols))
    sigma = jax.nn.sigmoid(preact)
    gfac[...] = sigma * (1.0 + preact * (1.0 - sigma))
    student = f96[hrows, ycols(y)].astype(F32) + preact * sigma
    sg[c, x, :, ycols(y)] = student.astype(BF16)
    step()
    arrive(
        [
            copy(sg.at[c, x, :, ycols(y)], sg.at[c, x, :, ycols(y)], dev(x_=xo(d)))
            for d in range(1, NX)
        ]
    )
    fwd = []

    def forward_s(i):
        fwd.append(copy(sg.at[c, :, :, ycols(i)], sg.at[c, :, :, ycols(i)], partner))

    for _ in gather_ring(ny, yo, dev(y_=yo(1)), dev(y_=yo(-1)), lambda i: sg.at[c, :, :, ycols(i)], forward_s):
        step()
    run(bg)
    ncp.wait_recv()
    voc = vg[...].reshape(d_model, vcols)
    logit_t = dot(f96[...], voc)
    logit_n = dot(fn[...], voc)
    arrive(fwd)
    n_st = NX * grp
    ls[0:n_st, :] = dot(sg[...].reshape(n_st, d_model), voc)
    ls[n_st : n_st + grp, :] = logit_t
    ls[n_st + grp : n_st + grp + 16, :] = logit_n
    ls[n_st + grp + 16 :, :] = jnp.zeros((16, vcols), F32)

    def reduce_plane(src, first_in, second_in):
        cps = [copy(src, first_in.at[x * 2 + c], dev(x_=a, c_=b)) for a, b in near]
        arrive(cps)
        row = src[...]
        for a, b in near:
            row = row + first_in[a * 2 + b]
        second_in[y] = row
        cps = [copy(second_in.at[y], second_in.at[y], dev(y_=yo(d))) for d in range(1, ny)]
        arrive(cps)
        row = second_in[0]
        for i in range(1, ny):
            row = row + second_in[i]
        return row

    ones = jnp.ones((8, vcols), F32)
    sums[...] = dot(ones, jnp.exp(ls[...]), ((1,), (1,)), HIGHEST)[0:1, :]
    logs = jnp.log(reduce_plane(sums, r1, r2))
    n_all = ls.shape[0]
    first_row = (iota((8, 128), 0) == 0).astype(F32)
    column = dot(jnp.broadcast_to(logs, (8, n_all)), first_row, ((0,), (0,)), HIGHEST)[:, 0:1]
    tl[...] = ls[n_st : n_st + tl.shape[0], :] - column[n_st : n_st + tl.shape[0]]
    losses = [None] * NX
    row_id = iota((hrow, 1), 0)
    n_tok = nz * grp
    for h in range(2):
        for k in range(NX):
            at = (h * NX + k) * hrow
            logp = ls[at : at + hrow, :] - column[at : at + hrow]
            target = tl[h * hrow + k + 1 : h * hrow + k + 1 + hrow, :]
            p = jnp.exp(target)
            weight = jnp.where(z * grp + h * hrow + row_id + (k + 1) < n_tok, 1.0 / (n_tok - k - 1), 0.0)
            terms = jnp.sum(weight * (p * (target - logp)), axis=0, keepdims=True)
            losses[k] = terms if losses[k] is None else losses[k] + terms
            sl[h, k * hrow : (k + 1) * hrow, :] = (weight * (jnp.exp(logp) - p)).astype(BF16)
    for k in range(NX):
        lsum[:, k * 128 : (k + 1) * 128] = losses[k][:, :128] + losses[k][:, 128:]

    got = {}
    for o in order:
        bs[yo(o)] = dot(sl[oc], vg[yo(o)], ((1,), (1,))).astype(BF16)
        got[o] = copy(bs.at[yo(o)], br.at[yo(o)], partner)
    for o in order:
        bo[yo(o)] = dot(sl[c], vg[yo(o)], ((1,), (1,)))
    total = scatter_ring(
        ny, yo, dev(y_=yo(1)), dev(y_=yo(-1)), lambda i: bo[i] + br[i].astype(F32), got, el, erl, er, err, lambda: None
    )
    xs2[...] = total.astype(BF16).reshape(xs2.shape)
    bcp = [copy(xs2.at[xo(d)], xr2.at[x], dev(x_=xo(d))) for d in range(1, NX)]
    arrive(tcp)
    turned = fw[...].reshape(nz * hrow, 256).astype(F32).T.astype(BF16)
    arrive(bcp)
    back = xs2[x].astype(F32)
    for d in range(1, NX):
        back = back + xr2[xo(d)].astype(F32)
    gg[z, x] = (back * gfac[...]).astype(BF16)

    arrive([copy(gg.at[z, x], gg.at[z, x], dev(x_=xo(d))) for d in range(1, NX)])
    ring = gather_ring(nz, zo, dev(z_=zo(1)), dev(z_=zo(-1)), lambda i: gg.at[i], nothing)
    next(ring)
    q3[z] = reduce_plane(lsum, q1, q2)
    lcp = [copy(q3.at[z], q3.at[z], dev(z_=zo(d))) for d in range(1, nz)]
    run(ring)

    cut = dp * vrow - jnp.minimum(lax.div(dp * vrow, 128) * 128, d_model - 256)
    oown[...] = turned
    lhs = oown[pl.ds(pl.multiple_of(cut, 32), vrow), :]
    cols = kcols // 2
    keep = []
    for k in range(NX):
        o = dot(lhs, gg[:, k].reshape(nz * hrow, kcols))
        low, high = o[:, :cols], o[:, cols:]
        osd[k] = jnp.where(c == 0, high, low)
        out_ref[k] = jnp.where(c == 0, low, high)
    ocp = copy(osd, ord_, partner)
    arrive(lcp)
    row = q3[0]
    for i in range(1, nz):
        row = row + q3[i]
    for k in range(NX):
        loss_ref[k] = jnp.sum(row[:, k * 128 : (k + 1) * 128])
    ocp.wait_recv()
    out_ref[...] = out_ref[...] + ord_[...]
    for cp in sent:
        cp.wait_send()


def solution(mesh):
    nz, ny = mesh.shape["dp"] // NX, mesh.shape["expert"] // 2

    def shards(tokens, routes, w_router, norm_gain, w_gate, w_up, w_down, final_gain, head_weights, vocab_proj):
        d_model = tokens.shape[1]
        half = d_model // 2
        kcols = d_model // ny
        vcols = vocab_proj.shape[1] // NX
        grp = NX * TOK
        hrow = grp // 2
        slots = NX * CAP
        vm = pltpu.VMEM
        scratch = [
            vm((d_model, 256), BF16),
            vm((2, 128, half), BF16),
            vm((nz, d_model // nz, vcols), BF16),
            vm((NX, hrow, kcols // 2), BF16),
            vm((NX, hrow, kcols), BF16),
            vm((nz, NX, 2, hrow, kcols), BF16),
            vm((2, TOK, half), BF16),
            vm((NX, SLOT, half), BF16),
            vm((2, nz, slots, half), BF16),
            vm((nz, slots, half), F32),
            vm((nz, slots, half), BF16),
            vm((nz, slots, half), BF16),
            vm((nz // 2, slots, half), BF16),
            vm((nz // 2, slots, half), BF16),
            vm((nz // 2, slots, half), BF16),
            vm((nz // 2, slots, half), BF16),
            vm((NX, SLOT, half), BF16),
            vm((NX, SLOT, half), BF16),
            vm((ny, SLOT, half), BF16),
            vm((2, TOK, 128), F32),
            vm((2, NX, 32, half), BF16),
            vm((grp, d_model), BF16),
            vm((nz, hrow, 256), BF16),
            vm((16, d_model), BF16),
            vm((hrow, kcols), F32),
            vm((2, NX, hrow, d_model), BF16),
            vm((512, vcols), F32),
            vm((grp + 16, vcols), F32),
            vm((1, 512), F32),
            vm((1, 512), F32),
            vm((2, NX * hrow, vcols), BF16),
            vm((ny, NX * hrow, kcols), F32),
            vm((ny, NX * hrow, kcols), BF16),
            vm((ny, NX * hrow, kcols), BF16),
            vm((ny // 2, NX * hrow, kcols), BF16),
            vm((ny // 2, NX * hrow, kcols), BF16),
            vm((ny // 2, NX * hrow, kcols), BF16),
            vm((ny // 2, NX * hrow, kcols), BF16),
            vm((NX, hrow, kcols), BF16),
            vm((NX, hrow, kcols), BF16),
            vm((nz, NX, hrow, kcols), BF16),
            vm((NX, 96, kcols // 2), F32),
            vm((NX, 96, kcols // 2), F32),
            vm((256, nz * hrow), BF16),
            vm((2 * NX, 1, 512), F32),
            vm((ny, 1, 512), F32),
            vm((2 * NX, 1, 512), F32),
            vm((ny, 1, 512), F32),
            vm((nz, 1, 512), F32),
            pltpu.SemaphoreType.DMA((N_COPIES,)),
            pltpu.SemaphoreType.DMA((N_COPIES,)),
            pltpu.SemaphoreType.DMA((8,)),
        ]

        def kernel(*refs):
            body(nz, ny, *refs)

        in_vmem = pl.BlockSpec(memory_space=pltpu.VMEM)
        in_hbm = pl.BlockSpec(memory_space=pl.ANY)
        losses, grads = pl.pallas_call(
            kernel,
            out_shape=(
                jax.ShapeDtypeStruct((NX,), F32),
                jax.ShapeDtypeStruct((NX, 96, kcols // 2), F32),
            ),
            in_specs=[in_vmem] * 6 + [in_hbm] * 4,
            out_specs=(pl.BlockSpec(memory_space=pltpu.SMEM), in_vmem),
            scratch_shapes=scratch,
            compiler_params=pltpu.CompilerParams(
                collective_id=0, has_side_effects=True, vmem_limit_bytes=60 * 2**20
            ),
            name="step",
        )(
            tokens,
            routes,
            w_router.T,
            norm_gain[None],
            final_gain[None],
            head_weights,
            w_gate[0],
            w_up[0],
            w_down[0],
            vocab_proj,
        )
        return losses, grads

    in_specs = (
        P("dp", None),
        P(),
        P(),
        P(),
        P("expert", None, "dp"),
        P("expert", None, "dp"),
        P("expert", "dp", None),
        P(),
        P(None, "dp", "expert"),
        P("dp", "expert"),
    )
    out_specs = (P(), P(None, "dp", "expert"))
    return jax.shard_map(shards, mesh=mesh, in_specs=in_specs, out_specs=out_specs, check_vma=False)
```

```python
import jax
import jax.numpy as jnp
from jax import lax
from jax.experimental import pallas as pl
from jax.experimental.pallas import tpu as pltpu
from jax.sharding import PartitionSpec as P

MESH = pl.DeviceIdType.MESH
F32, BF16 = jnp.float32, jnp.bfloat16
HIGHEST = lax.Precision.HIGHEST
EPS = 1e-05
NX = 4
TOK, CAP, SLOT = 24, 12, 16
N_COPIES = 480
ROWS = 48
ALL = slice(None)
NEAR, FAR = slice(0, 16), slice(16, 48)


def dot(a, b, dims=((1,), (0,)), precision=None):
    return lax.dot_general(a, b, (dims, ((), ())), precision=precision, preferred_element_type=F32)


def iota(shape, axis):
    return lax.broadcasted_iota(jnp.int32, shape, axis)


def pump(*tasks):
    live = list(tasks)
    while live:
        live = [task for task in live if next(task, live) is not live]


def body(
    nz, ny, tok_ref, routes_ref, wr_ref, ng_ref, fg_ref, hw_ref, wg_hbm, wu_hbm, wd_hbm, voc_hbm, loss_ref, out_ref,
    w_gu, wd, vg, hx, hl, hg, tk, tokf, nbs, ag, yg, uq, f96, fw, fn, gfac, sg,
    ls, tl, sums, lsum, sl, gg, osd, ord_, lhs_t, s1, s2, r1, r2, q1, q2, q3, dset, hset,
    ss, rs, lsem,
):
    dp, ex = lax.axis_index("dp"), lax.axis_index("expert")
    z, x = lax.div(dp, NX), lax.rem(dp, NX)
    y, c = lax.div(ex, 2), lax.rem(ex, 2)
    oc = 1 - c
    d_model = tok_ref.shape[1]
    half = d_model // 2
    vcols = vg.shape[2]
    kcols = d_model // ny
    grp = NX * TOK
    n_exp = wr_ref.shape[0]

    def dev(z_=None, x_=None, y_=None, c_=None):
        z_, x_ = (z if z_ is None else z_), (x if x_ is None else x_)
        y_, c_ = (y if y_ is None else y_), (c if c_ is None else c_)
        return {"dp": z_ * NX + x_, "expert": y_ * 2 + c_}

    def xo(d):
        return lax.rem(x + (d + NX), NX)

    def zo(d):
        return lax.rem(z + (d + nz), nz)

    def yo(d):
        return lax.rem(y + (d + ny), ny)

    partner = dev(c_=oc)
    over_x = [dev(x_=xo(d)) for d in range(1, NX)]
    sign = 1 - 2 * c
    z_ring = (nz, zo, lambda d: dev(z_=zo(d)))
    y_ring = (ny, yo, lambda d: dev(y_=yo(d)))
    sent = []

    def copy(src, dst, device):
        i = len(sent)
        cp = pltpu.make_async_remote_copy(
            src_ref=src, dst_ref=dst, send_sem=ss.at[i], recv_sem=rs.at[i], device_id=device, device_id_type=MESH
        )
        cp.start()
        sent.append(cp)
        return cp

    def same(ref, device):
        return copy(ref, ref, device)

    locals_ = []

    def local(src, dst):
        cp = pltpu.make_async_copy(src, dst, lsem.at[len(locals_)])
        cp.start()
        locals_.append(cp)
        return cp

    def arrive(copies):
        for cp in copies:
            cp.wait_recv()

    vrow = d_model // (nz * NX)
    quarter = lambda x_: pl.ds(pl.multiple_of(x_ * vcols, 128), vcols)
    hcols = lambda c_: pl.ds(pl.multiple_of(c_ * half, 128), half)
    ycols = lambda y_: pl.ds(pl.multiple_of(y_ * kcols, 128), kcols)
    vslot = lambda x_: pl.ds(pl.multiple_of(x_ * vrow, 16), vrow)
    in_w = [
        local(wg_hbm, w_gu.at[:, 0:128]),
        local(wu_hbm, w_gu.at[:, 128:256]),
        local(wd_hbm.at[:, hcols(c)], wd.at[0]),
        local(wd_hbm.at[:, hcols(oc)], wd.at[1]),
    ]
    in_v = local(voc_hbm.at[:, quarter(x)], vg.at[z, vslot(x), :])

    barrier = pltpu.get_barrier_semaphore()
    line_z = [dev(z_=zo(d)) for d in range(1, nz)]
    line_y = [dev(y_=yo(d)) for d in range(1, ny)]
    near = [(xo(d), c_) for d in range(1, NX) for c_ in (c, oc)] + [(x, oc)]
    plane = [dev(x_=a, c_=b) for a, b in near]
    peers = line_z + line_y + plane
    for peer in peers:
        pl.semaphore_signal(barrier, inc=1, device_id=peer, device_id_type=MESH)
    tk[c, x] = tok_ref[:, hcols(c)]
    tk[oc, x] = tok_ref[:, hcols(oc)]
    pl.semaphore_wait(barrier, len(peers))

    tcp = [copy(tok_ref.at[:, hcols(c)], tk.at[c, x], peer) for peer in over_x]

    def ring_gather(at, ring, on_arrival):
        n, off, to = ring
        h = n // 2
        a, b = same(at(off(0)), to(1)), same(at(off(0)), to(-1))
        for s in range(1, h + 1):
            yield
            a.wait_recv()
            if s < h:
                a = same(at(off(-s)), to(1))
            on_arrival(off(-s))
            if s < h:
                b.wait_recv()
                if s < h - 1:
                    b = same(at(off(s)), to(-1))
                on_arrival(off(s))

    def two_step_gather(at, ring, on_arrival):
        _, off, to = ring
        cps = {o: same(at(off(0)), to(o)) for o in (2, -2, 1, -1)}
        yield
        cps[2].wait_recv()
        cps[3] = same(at(off(-2)), to(1))
        cps[-2].wait_recv()
        cps[-3] = same(at(off(2)), to(-1))
        cps[4] = same(at(off(-2 * sign)), to(2 * sign))
        for o in (2, -2):
            on_arrival(off(-o))
        for o in (1, -1):
            cps[o].wait_recv()
            on_arrival(off(-o))
        yield
        for o in (3, -3, 4):
            cps[o].wait_recv()
            on_arrival(off(-o))

    def gather(at, ring, on_arrival=None, hooks=(), skip_x=False):
        _, off, to = ring
        take = on_arrival or (lambda ref: None)
        hooks = list(hooks)

        def hook():
            if hooks:
                hooks.pop(0)()

        on_x = []

        def over(o):
            ref = at(off(o), x, FAR)
            on_x.append((off(o), [same(ref, peer) for peer in over_x]))
            take(ref)

        bundle = lambda i: at(i, ALL, NEAR)
        near = two_step_gather(bundle, ring, lambda i: take(bundle(i)))
        cps = {o: same(at(off(0), x, FAR), to(o)) for o in (1, -1, 2, -2, 3, -3, 4)}
        if skip_x:
            take(bundle(off(0)))
            step(near)
        else:
            x_cps = [same(at(off(0), x, NEAR), peer) for peer in over_x]
        over(0)
        hook()
        for o, cp in cps.items():
            cp.wait_recv()
            over(-o)
            if o == -1 and not skip_x:
                arrive(x_cps)
                take(bundle(off(0)))
                step(near)
        hook()
        step(near)
        hook()
        for i, by_peer in on_x:
            for d, cp in zip(range(1, NX), by_peer):
                cp.wait_recv()
                take(at(i, xo(NX - d), FAR))
        hook()
        step(near)
        while hooks:
            hook()

    def scatter(fill, ring, bufs, hooks=()):
        po, ps, pr, x1s, x1r, zs, zr = bufs
        n, off, to = ring
        order = (4, 3, -3, 2, -2, 1, -1, 0)
        hooks = list(hooks)

        def hook():
            if hooks:
                hooks.pop(0)()

        fill(ps, oc)
        got = {o: copy(ps.at[off(o)], pr.at[off(o)], partner) for o in order}
        fill(po, c)
        cps = {}
        way = {o: (1, -1)[k % 2] for k, o in enumerate(order)}

        def own(o, j):
            return po[off(o), j] + pr[off(o), j].astype(F32)

        def send(i, o, value, d):
            x1s[i, off(o)] = value.astype(BF16)
            cps[i, o] = copy(x1s.at[i, off(o)], x1r.at[i, off(o)], dev(x_=xo(d)))

        def out(o):
            got[o].wait_recv()
            send(0, o, own(o, xo(2)), way[o])
            send(1, o, own(o, xo(-way[o])), -way[o])

        def middle(o):
            cps[0, o].wait_recv()
            send(2, o, own(o, xo(way[o])) + x1r[0, off(o)].astype(F32), way[o])

        def term(o):
            value = own(o, x)
            for i in (1, 2):
                cps[i, o].wait_recv()
                value = value + x1r[i, off(o)].astype(F32)
            return value

        last = []

        def along(o):
            zs[o % n] = term(o).astype(BF16)
            last.append(copy(zs.at[o % n], zr.at[o % n], to(o)))

        for o in order[:4]:
            out(o)
        hook()
        for o, later in zip(order[:4], order[4:]):
            out(later)
            middle(o)
        hook()
        for o, later in zip(order[:4], order[4:]):
            along(o)
            middle(later)
        for o in order[4:-1]:
            along(o)
        value = term(0)
        hook()
        arrive(last)
        for o in order[:-1]:
            value = value + zr[o % n].astype(F32)
        while hooks:
            hook()
        return value

    nothing = lambda *_: None

    hrows = lambda c_: pl.ds(pl.multiple_of(c_ * ROWS, 16), ROWS)
    vx = [copy(voc_hbm.at[:, quarter(xo(d))], vg.at[z, vslot(x), :], peer) for d, peer in zip(range(1, NX), over_x)]
    ex_h = copy(hw_ref.at[:, hrows(oc), :], hx, partner)

    def heads():
        ex_h.wait_recv()
        for k in range(NX):
            mine, theirs = hw_ref[k, hrows(c), :], hx[k]
            left = jnp.where(c == 0, mine, theirs)
            right = jnp.where(c == 0, theirs, mine)
            hl[k] = jnp.concatenate([left, right], axis=1)
        cps = [copy(hl.at[xo(d)], hg.at[z, x, c], peer) for d, peer in zip(range(1, NX), over_x)]
        hg[z, x, c] = hl[x]
        yield
        arrive(cps)
        forwards = []

        def forward(i):
            forwards.append(same(hg.at[i, :, c], partner))

        forward(z)
        yield from ring_gather(lambda i: hg.at[i, :, c], z_ring, forward)
        yield
        arrive(forwards)

    def vocabulary():
        arrive(vx)
        in_v.wait()
        yield from ring_gather(lambda i: vg.at[i], z_ring, nothing)

    heads, vocabulary = heads(), vocabulary()
    step = lambda task: next(task, None)

    fwd = []
    for d, cp in zip(range(1, NX), tcp):
        cp.wait_recv()
        src = xo(NX - d)
        fwd.append(same(tk.at[c, src], partner))
    pick_rows = (iota((grp, nz * grp), 1) == iota((grp, nz * grp), 0) + z * grp).astype(BF16)
    own_routes = dot(pick_rows, routes_ref[...].astype(F32).astype(BF16), ((1,), (1,)))
    e0, e1 = own_routes[:, 0:1], own_routes[:, 1:2]
    row_t = iota((grp, 1), 0)
    block = (row_t >= TOK).astype(jnp.int32) + (row_t >= 2 * TOK).astype(jnp.int32) + (row_t >= 3 * TOK).astype(jnp.int32)
    col_t = iota((grp, grp), 1)
    lower = jnp.logical_and(col_t < row_t, col_t >= block * TOK).astype(F32).astype(BF16)
    lane_e = iota((grp, n_exp), 1).astype(F32)
    hot0, hot1 = (e0 == lane_e).astype(F32), (e1 == lane_e).astype(F32)
    earlier = dot(lower, (hot0 + hot1).astype(BF16))
    at_block = (block * CAP).astype(F32)
    place0 = e0 * ROWS + at_block + jnp.sum(hot0 * earlier, axis=1, keepdims=True)
    place1 = e1 * ROWS + at_block + jnp.sum(hot1 * earlier, axis=1, keepdims=True)
    own_slot = (iota((grp, ROWS), 1) + y * ROWS).astype(F32)
    select = ((place0 == own_slot).astype(F32) + (place1 == own_slot).astype(F32)).astype(BF16)
    arrive(fwd)
    square = jnp.zeros((grp, 1), F32)
    for h in range(2):
        rows = tk[h].astype(F32).reshape(grp, half)
        square = square + jnp.sum(rows * rows, axis=1, keepdims=True)
        for j in range(NX):
            tokf[h * NX + j] = rows[:, j * kcols : (j + 1) * kcols]
    scale = lax.rsqrt(square * (1.0 / d_model) + EPS)
    router = jnp.zeros((grp, n_exp), F32)
    for i in range(2 * NX):
        cols = slice(i * kcols, (i + 1) * kcols)
        normed = (tokf[i] * scale * ng_ref[:, cols]).astype(BF16)
        nbs[i] = normed
        router = router + dot(normed, wr_ref[:, cols], ((1,), (1,)))
    for j in range(NX):
        ag[c, z, j, NEAR] = dot(select[:, NEAR], nbs[c * NX + j], ((0,), (0,))).astype(BF16)
    ag[c, z, x, FAR] = dot(select[:, FAR], nbs[c * NX + x], ((0,), (0,))).astype(BF16)

    fwd = []
    forward = lambda ref: fwd.append(same(ref, partner))
    more = lambda: step(heads)
    gather(lambda i, j, rows: ag.at[c, i, j, rows], z_ring, forward, [more, nothing, more, more], skip_x=True)
    first = jax.nn.sigmoid(jnp.sum(router * (hot0 - hot1), axis=1, keepdims=True))
    lane_f = iota((grp, n_exp * ROWS), 1).astype(F32)
    weigh = first * (place0 == lane_f).astype(F32) + (1.0 - first) * (place1 == lane_f).astype(F32)
    weigh_hi = weigh.astype(BF16)
    weigh_lo = (weigh - weigh_hi.astype(F32)).astype(BF16)
    arrive(fwd)
    for cp in in_w:
        cp.wait()

    n_rows = nz * ROWS
    pre = jnp.zeros((n_rows, 256), F32)
    for h in range(2):
        for j in range(NX):
            i = h * NX + j
            pre = pre + dot(ag[h, :, j].reshape(n_rows, kcols), w_gu[i * kcols : (i + 1) * kcols, :])
    hidden = (jax.nn.silu(pre[:, :128]) * pre[:, 128:]).astype(BF16)
    step(heads)

    def fill_rows(dst, core):
        w = wd.at[0 if core is c else 1]
        for j in range(NX):
            value = dot(hidden, w[:, j * kcols : (j + 1) * kcols])
            dst[:, j] = value.astype(dst.dtype).reshape(nz, ROWS, kcols)

    total = scatter(fill_rows, z_ring, dset, [more, lambda: pump(heads)])
    step(vocabulary)

    yg[y] = total.astype(BF16)
    across = two_step_gather(lambda i: yg.at[i], y_ring, lambda i: None)
    pump(across)
    step(vocabulary)
    outs = yg[...].reshape(n_exp * ROWS, kcols)
    mixed = tokf[c * NX + x] + dot(weigh_hi, outs) + dot(weigh_lo, outs)
    square = dot(jnp.ones((8, kcols), F32), mixed * mixed, ((1,), (1,)), HIGHEST)
    s1[:, 0:grp] = square[0:1, :]
    s1[:, grp:] = jnp.zeros((1, 128 - grp), F32)
    uq[c, x] = mixed.astype(BF16)
    ucp = [same(uq.at[c, x], peer) for peer in over_x]
    scp = [copy(s1, s2.at[x * 2 + c], peer) for peer in plane]
    fwd = [same(uq.at[c, x], partner)]
    step(heads)
    for d, cp in zip(range(1, NX), ucp):
        cp.wait_recv()
        fwd.append(same(uq.at[c, xo(NX - d)], partner))
    step(vocabulary)
    arrive(scp)
    square = s1[...]
    for a, b in near:
        square = square + s2[a * 2 + b]
    first_row = (iota((8, 128), 0) == 0).astype(F32)
    scale = lax.rsqrt(square * (1.0 / d_model) + EPS)
    scale = dot(jnp.broadcast_to(scale, (8, 128)), first_row, ((0,), (0,)), HIGHEST)[0:grp, 0:1]
    arrive(fwd)
    for h in range(2):
        for j in range(NX):
            i = h * NX + j
            cols = slice(i * kcols, (i + 1) * kcols)
            f96[:, cols] = (uq[h, j].astype(F32) * scale * fg_ref[:, cols]).astype(BF16)

    def window(z_):
        start = jnp.minimum(lax.div((z_ * NX + x) * vrow, 128) * 128, d_model - 256)
        return pl.ds(pl.multiple_of(start, 128), 256)

    tcp = [copy(f96.at[hrows(c), window(zo(d))], fw.at[z], peer) for d, peer in zip(range(1, nz), line_z)]
    fw[z] = f96[hrows(c), window(z)]
    ncp = copy(f96.at[0:16, :], fn, dev(z_=zo(-1)))

    pump(heads)
    preact = dot(f96[hrows(c), :], hg[...].reshape(d_model, kcols))
    sigma = jax.nn.sigmoid(preact)
    gfac[...] = sigma * (1.0 + preact * (1.0 - sigma))
    student = f96[hrows(c), ycols(y)].astype(F32) + preact * sigma
    sg[c, x, :, ycols(y)] = student.astype(BF16)

    fwd = []
    part = lambda i, j, rows: sg.at[c, j, rows, ALL if i is ALL else ycols(i)]
    gather(part, y_ring, forward_to(fwd, same, partner), [nothing, lambda: step(vocabulary)])
    pump(vocabulary)
    ncp.wait_recv()
    voc = vg[...].reshape(d_model, vcols)
    n_st = NX * grp
    ls[n_st : n_st + grp, :] = dot(f96[...], voc)
    ls[n_st + grp : n_st + grp + 16, :] = dot(fn[...], voc)
    ls[n_st + grp + 16 :, :] = jnp.zeros((16, vcols), F32)
    arrive(fwd)
    ls[0:n_st, :] = dot(sg[...].reshape(n_st, d_model), voc)

    def reduce_plane(src, first_in, second_in, result):
        cps = [copy(src, first_in.at[x * 2 + c], peer) for peer in plane]
        yield
        arrive(cps)
        row = src[...]
        for a, b in near:
            row = row + first_in[a * 2 + b]
        second_in[y] = row
        cps = [same(second_in.at[y], peer) for peer in line_y]
        yield
        arrive(cps)
        row = second_in[0]
        for i in range(1, ny):
            row = row + second_in[i]
        result.append(row)

    ones = jnp.ones((8, vcols), F32)
    sums[...] = dot(ones, jnp.exp(ls[...]), ((1,), (1,)), HIGHEST)[0:1, :]
    result = []
    pump(reduce_plane(sums, r1, r2, result))
    logs = jnp.log(result[0])
    n_all = ls.shape[0]
    column = dot(jnp.broadcast_to(logs, (8, n_all)), first_row, ((0,), (0,)), HIGHEST)[:, 0:1]
    tl[...] = ls[n_st : n_st + tl.shape[0], :] - column[n_st : n_st + tl.shape[0]]
    losses = [None] * NX
    row_id = iota((ROWS, 1), 0)
    n_tok = nz * grp
    for h in range(2):
        for k in range(NX):
            at = (h * NX + k) * ROWS
            logp = ls[at : at + ROWS, :] - column[at : at + ROWS]
            target = tl[h * ROWS + k + 1 : h * ROWS + k + 1 + ROWS, :]
            p = jnp.exp(target)
            weight = jnp.where(z * grp + h * ROWS + row_id + (k + 1) < n_tok, 1.0 / (n_tok - k - 1), 0.0)
            terms = jnp.sum(weight * (p * (target - logp)), axis=0, keepdims=True)
            losses[k] = terms if losses[k] is None else losses[k] + terms
            sl[h, k * ROWS : (k + 1) * ROWS, :] = (weight * (jnp.exp(logp) - p)).astype(BF16)
    for k in range(NX):
        lsum[:, k * 128 : (k + 1) * 128] = losses[k][:, :128] + losses[k][:, 128:]

    def fill_back(dst, core):
        for i in range(ny):
            value = dot(sl[core], vg[i], ((1,), (1,)))
            dst[i] = value.astype(dst.dtype).reshape(NX, ROWS, kcols)

    back = scatter(fill_back, y_ring, hset)
    gg[z, x] = (back * gfac[...]).astype(BF16)

    loss_rows = []

    def loss_task():
        result = []
        yield from reduce_plane(lsum, q1, q2, result)
        q3[z] = result[0]
        cps = [same(q3.at[z], peer) for peer in line_z]
        yield
        arrive(cps)
        row = q3[0]
        for i in range(1, nz):
            row = row + q3[i]
        loss_rows.append(row)

    def turn():
        arrive(tcp)
        lhs_t[...] = fw[...].reshape(nz * ROWS, 256).astype(F32).T.astype(BF16)

    task = loss_task()
    go_on = lambda: step(task)
    gather(lambda i, j, rows: gg.at[i, j, rows], z_ring, None, [lambda: (go_on(), turn()), go_on, go_on, go_on])

    cut = dp * vrow - jnp.minimum(lax.div(dp * vrow, 128) * 128, d_model - 256)
    lhs = lhs_t[pl.ds(pl.multiple_of(cut, 32), vrow), :]
    cols = kcols // 2
    for k in range(NX):
        o = dot(lhs, gg[:, k].reshape(nz * ROWS, kcols))
        low, high = o[:, :cols], o[:, cols:]
        osd[k] = jnp.where(c == 0, high, low)
        out_ref[k] = jnp.where(c == 0, low, high)
    ocp = copy(osd, ord_, partner)
    row = loss_rows[0]
    for k in range(NX):
        loss_ref[k] = jnp.sum(row[:, k * 128 : (k + 1) * 128])
    ocp.wait_recv()
    out_ref[...] = out_ref[...] + ord_[...]
    for cp in sent:
        cp.wait_send()


def forward_to(forwards, same, partner):
    return lambda ref: forwards.append(same(ref, partner))


def solution(mesh):
    nz, ny = mesh.shape["dp"] // NX, mesh.shape["expert"] // 2

    def shards(tokens, routes, w_router, norm_gain, w_gate, w_up, w_down, final_gain, head_weights, vocab_proj):
        d_model = tokens.shape[1]
        half = d_model // 2
        kcols = d_model // ny
        vcols = vocab_proj.shape[1] // NX
        grp = NX * TOK
        vm = pltpu.VMEM

        def scatter_set(n, own):
            return (
                vm((n, NX, ROWS, kcols), own),
                vm((n, NX, ROWS, kcols), BF16),
                vm((n, NX, ROWS, kcols), BF16),
                vm((NX - 1, n, ROWS, kcols), BF16),
                vm((NX - 1, n, ROWS, kcols), BF16),
                vm((n, ROWS, kcols), BF16),
                vm((n, ROWS, kcols), BF16),
            )

        flat = [
            vm((d_model, 256), BF16),
            vm((2, 128, half), BF16),
            vm((nz, d_model // nz, vcols), BF16),
            vm((NX, ROWS, kcols // 2), BF16),
            vm((NX, ROWS, kcols), BF16),
            vm((nz, NX, 2, ROWS, kcols), BF16),
            vm((2, NX, TOK, half), BF16),
            vm((2 * NX, grp, kcols), F32),
            vm((2 * NX, grp, kcols), BF16),
            vm((2, nz, NX, ROWS, kcols), BF16),
            vm((ny, ROWS, kcols), BF16),
            vm((2, NX, grp, kcols), BF16),
            vm((grp, d_model), BF16),
            vm((nz, ROWS, 256), BF16),
            vm((16, d_model), BF16),
            vm((ROWS, kcols), F32),
            vm((2, NX, ROWS, d_model), BF16),
            vm((512, vcols), F32),
            vm((grp + 16, vcols), F32),
            vm((1, 512), F32),
            vm((1, 512), F32),
            vm((2, NX * ROWS, vcols), BF16),
            vm((nz, NX, ROWS, kcols), BF16),
            vm((NX, 96, kcols // 2), F32),
            vm((NX, 96, kcols // 2), F32),
            vm((256, nz * ROWS), BF16),
            vm((1, 128), F32),
            vm((2 * NX, 1, 128), F32),
            vm((2 * NX, 1, 512), F32),
            vm((ny, 1, 512), F32),
            vm((2 * NX, 1, 512), F32),
            vm((ny, 1, 512), F32),
            vm((nz, 1, 512), F32),
        ]
        scratch = flat + [
            scatter_set(nz, F32),
            scatter_set(ny, F32),
            pltpu.SemaphoreType.DMA((N_COPIES,)),
            pltpu.SemaphoreType.DMA((N_COPIES,)),
            pltpu.SemaphoreType.DMA((8,)),
        ]

        def kernel(*refs):
            body(nz, ny, *refs)

        in_vmem = pl.BlockSpec(memory_space=pltpu.VMEM)
        in_hbm = pl.BlockSpec(memory_space=pl.ANY)
        losses, grads = pl.pallas_call(
            kernel,
            out_shape=(
                jax.ShapeDtypeStruct((NX,), F32),
                jax.ShapeDtypeStruct((NX, 96, kcols // 2), F32),
            ),
            in_specs=[in_vmem] * 6 + [in_hbm] * 4,
            out_specs=(pl.BlockSpec(memory_space=pltpu.SMEM), in_vmem),
            scratch_shapes=scratch,
            compiler_params=pltpu.CompilerParams(
                collective_id=0, has_side_effects=True, vmem_limit_bytes=60 * 2**20
            ),
            name="step",
        )(
            tokens,
            routes.T,
            w_router.T,
            norm_gain[None],
            final_gain[None],
            head_weights,
            w_gate[0],
            w_up[0],
            w_down[0],
            vocab_proj,
        )
        return losses, grads

    in_specs = (
        P("dp", None),
        P(),
        P(),
        P(),
        P("expert", None, "dp"),
        P("expert", None, "dp"),
        P("expert", "dp", None),
        P(),
        P(None, "dp", "expert"),
        P("dp", "expert"),
    )
    out_specs = (P(), P(None, "dp", "expert"))
    return jax.shard_map(shards, mesh=mesh, in_specs=in_specs, out_specs=out_specs, check_vma=False)
```

```python
import jax
import jax.numpy as jnp
from jax import lax
from jax.experimental import pallas as pl
from jax.experimental.pallas import tpu as pltpu
from jax.sharding import PartitionSpec as P

MESH = pl.DeviceIdType.MESH
F32, BF16 = jnp.float32, jnp.bfloat16
HIGHEST = lax.Precision.HIGHEST
EPS = 1e-05
NX = 4
TOK, CAP, SLOT = 24, 12, 16
N_COPIES = 480
ROWS = 48
ALL = slice(None)
NEAR, FAR = slice(0, 16), slice(16, 48)


def dot(a, b, dims=((1,), (0,)), precision=None):
    return lax.dot_general(a, b, (dims, ((), ())), precision=precision, preferred_element_type=F32)


def iota(shape, axis):
    return lax.broadcasted_iota(jnp.int32, shape, axis)


def pump(*tasks):
    live = list(tasks)
    while live:
        live = [task for task in live if next(task, live) is not live]


def body(
    nz, ny, tok_hbm, routes_hbm, wr_hbm, ng_hbm, fg_hbm, hw_hbm, wg_hbm, wu_hbm, wd_hbm, voc_hbm, loss_ref, out_ref,
    tok_ref, routes_ref, wr_ref, ng_ref, fg_ref, hw_ref, w_gu, wd, vg, hx, hl, hg, tk, tokf, nbs, ag, yg, uq, f96, fw, fn, gfac, sg,
    ls, tl, sums, lsum, sl, gg, osd, ord_, lhs_t, s1, s2, r1, r2, q1, q2, q3, dset, hset,
    ss, rs, lsem,
):
    dp, ex = lax.axis_index("dp"), lax.axis_index("expert")
    z, x = lax.div(dp, NX), lax.rem(dp, NX)
    y, c = lax.div(ex, 2), lax.rem(ex, 2)
    oc = 1 - c
    d_model = tok_ref.shape[1]
    half = d_model // 2
    vcols = vg.shape[2]
    kcols = d_model // ny
    grp = NX * TOK
    n_exp = wr_ref.shape[0]

    def dev(z_=None, x_=None, y_=None, c_=None):
        z_, x_ = (z if z_ is None else z_), (x if x_ is None else x_)
        y_, c_ = (y if y_ is None else y_), (c if c_ is None else c_)
        return {"dp": z_ * NX + x_, "expert": y_ * 2 + c_}

    def xo(d):
        return lax.rem(x + (d + NX), NX)

    def zo(d):
        return lax.rem(z + (d + nz), nz)

    def yo(d):
        return lax.rem(y + (d + ny), ny)

    partner = dev(c_=oc)
    over_x = [dev(x_=xo(d)) for d in range(1, NX)]
    sign = 1 - 2 * c
    z_ring = (nz, zo, lambda d: dev(z_=zo(d)))
    y_ring = (ny, yo, lambda d: dev(y_=yo(d)))
    sent = []

    def copy(src, dst, device):
        i = len(sent)
        cp = pltpu.make_async_remote_copy(
            src_ref=src, dst_ref=dst, send_sem=ss.at[i], recv_sem=rs.at[i], device_id=device, device_id_type=MESH
        )
        cp.start()
        sent.append(cp)
        return cp

    def same(ref, device):
        return copy(ref, ref, device)

    locals_ = []

    def local(src, dst):
        cp = pltpu.make_async_copy(src, dst, lsem.at[len(locals_)])
        cp.start()
        locals_.append(cp)
        return cp

    def arrive(copies):
        for cp in copies:
            cp.wait_recv()

    vrow = d_model // (nz * NX)
    quarter = lambda x_: pl.ds(pl.multiple_of(x_ * vcols, 128), vcols)
    hcols = lambda c_: pl.ds(pl.multiple_of(c_ * half, 128), half)
    ycols = lambda y_: pl.ds(pl.multiple_of(y_ * kcols, 128), kcols)
    vslot = lambda x_: pl.ds(pl.multiple_of(x_ * vrow, 16), vrow)
    in_tok = local(tok_hbm, tok_ref)
    in_small = [
        local(src, dst)
        for src, dst in (
            (routes_hbm, routes_ref),
            (wr_hbm, wr_ref),
            (ng_hbm, ng_ref),
            (fg_hbm, fg_ref),
            (hw_hbm, hw_ref),
        )
    ]
    in_w = [
        local(wg_hbm, w_gu.at[:, 0:128]),
        local(wu_hbm, w_gu.at[:, 128:256]),
        local(wd_hbm.at[:, hcols(c)], wd.at[0]),
        local(wd_hbm.at[:, hcols(oc)], wd.at[1]),
    ]
    in_v = local(voc_hbm.at[:, quarter(x)], vg.at[z, vslot(x), :])

    barrier = pltpu.get_barrier_semaphore()
    line_z = [dev(z_=zo(d)) for d in range(1, nz)]
    line_y = [dev(y_=yo(d)) for d in range(1, ny)]
    near = [(xo(d), c_) for d in range(1, NX) for c_ in (c, oc)] + [(x, oc)]
    plane = [dev(x_=a, c_=b) for a, b in near]
    peers = line_z + line_y + plane
    for peer in peers:
        pl.semaphore_signal(barrier, inc=1, device_id=peer, device_id_type=MESH)
    in_tok.wait()
    tk[c, x] = tok_ref[:, hcols(c)]
    tk[oc, x] = tok_ref[:, hcols(oc)]
    pl.semaphore_wait(barrier, len(peers))

    tcp = [copy(tok_ref.at[:, hcols(c)], tk.at[c, x], peer) for peer in over_x]

    def ring_gather(at, ring, on_arrival):
        n, off, to = ring
        h = n // 2
        a, b = same(at(off(0)), to(1)), same(at(off(0)), to(-1))
        for s in range(1, h + 1):
            yield
            a.wait_recv()
            if s < h:
                a = same(at(off(-s)), to(1))
            on_arrival(off(-s))
            if s < h:
                b.wait_recv()
                if s < h - 1:
                    b = same(at(off(s)), to(-1))
                on_arrival(off(s))

    def two_step_gather(at, ring, on_arrival):
        _, off, to = ring
        cps = {o: same(at(off(0)), to(o)) for o in (2, -2, 1, -1)}
        yield
        cps[2].wait_recv()
        cps[3] = same(at(off(-2)), to(1))
        cps[-2].wait_recv()
        cps[-3] = same(at(off(2)), to(-1))
        cps[4] = same(at(off(-2 * sign)), to(2 * sign))
        for o in (2, -2):
            on_arrival(off(-o))
        for o in (1, -1):
            cps[o].wait_recv()
            on_arrival(off(-o))
        yield
        for o in (3, -3, 4):
            cps[o].wait_recv()
            on_arrival(off(-o))

    def gather(at, ring, on_arrival=None, hooks=(), skip_x=False):
        _, off, to = ring
        take = on_arrival or (lambda ref: None)
        hooks = list(hooks)

        def hook():
            if hooks:
                hooks.pop(0)()

        on_x = []

        def over(o):
            ref = at(off(o), x, FAR)
            on_x.append((off(o), [same(ref, peer) for peer in over_x]))
            take(ref)

        bundle = lambda i: at(i, ALL, NEAR)
        near = two_step_gather(bundle, ring, lambda i: take(bundle(i)))
        cps = {o: same(at(off(0), x, FAR), to(o)) for o in (1, -1, 2, -2, 3, -3, 4)}
        if skip_x:
            take(bundle(off(0)))
            step(near)
        else:
            x_cps = [same(at(off(0), x, NEAR), peer) for peer in over_x]
        over(0)
        hook()
        for o, cp in cps.items():
            cp.wait_recv()
            over(-o)
            if o == -1 and not skip_x:
                arrive(x_cps)
                take(bundle(off(0)))
                step(near)
        hook()
        step(near)
        hook()
        for i, by_peer in on_x:
            for d, cp in zip(range(1, NX), by_peer):
                cp.wait_recv()
                take(at(i, xo(NX - d), FAR))
        hook()
        step(near)
        while hooks:
            hook()

    def scatter(fill, ring, bufs, hooks=()):
        po, ps, pr, x1s, x1r, zs, zr = bufs
        n, off, to = ring
        order = (4, 3, -3, 2, -2, 1, -1, 0)
        hooks = list(hooks)

        def hook():
            if hooks:
                hooks.pop(0)()

        fill(ps, oc)
        got = {o: copy(ps.at[off(o)], pr.at[off(o)], partner) for o in order}
        fill(po, c)
        cps = {}
        way = {o: (1, -1)[k % 2] for k, o in enumerate(order)}

        def own(o, j):
            return po[off(o), j] + pr[off(o), j].astype(F32)

        def send(i, o, value, d):
            x1s[i, off(o)] = value.astype(BF16)
            cps[i, o] = copy(x1s.at[i, off(o)], x1r.at[i, off(o)], dev(x_=xo(d)))

        def out(o):
            got[o].wait_recv()
            send(0, o, own(o, xo(2)), way[o])
            send(1, o, own(o, xo(-way[o])), -way[o])

        def middle(o):
            cps[0, o].wait_recv()
            send(2, o, own(o, xo(way[o])) + x1r[0, off(o)].astype(F32), way[o])

        def term(o):
            value = own(o, x)
            for i in (1, 2):
                cps[i, o].wait_recv()
                value = value + x1r[i, off(o)].astype(F32)
            return value

        last = []

        def along(o):
            zs[o % n] = term(o).astype(BF16)
            last.append(copy(zs.at[o % n], zr.at[o % n], to(o)))

        for o in order[:4]:
            out(o)
        hook()
        for o, later in zip(order[:4], order[4:]):
            out(later)
            middle(o)
        hook()
        for o, later in zip(order[:4], order[4:]):
            along(o)
            middle(later)
        for o in order[4:-1]:
            along(o)
        value = term(0)
        hook()
        arrive(last)
        for o in order[:-1]:
            value = value + zr[o % n].astype(F32)
        while hooks:
            hook()
        return value

    nothing = lambda *_: None

    hrows = lambda c_: pl.ds(pl.multiple_of(c_ * ROWS, 16), ROWS)
    vx = [copy(voc_hbm.at[:, quarter(xo(d))], vg.at[z, vslot(x), :], peer) for d, peer in zip(range(1, NX), over_x)]
    ex_h = copy(hw_hbm.at[:, hrows(oc), :], hx, partner)

    def heads():
        ex_h.wait_recv()
        for k in range(NX):
            mine, theirs = hw_ref[k, hrows(c), :], hx[k]
            left = jnp.where(c == 0, mine, theirs)
            right = jnp.where(c == 0, theirs, mine)
            hl[k] = jnp.concatenate([left, right], axis=1)
        cps = [copy(hl.at[xo(d)], hg.at[z, x, c], peer) for d, peer in zip(range(1, NX), over_x)]
        hg[z, x, c] = hl[x]
        yield
        arrive(cps)
        forwards = []

        def forward(i):
            forwards.append(same(hg.at[i, :, c], partner))

        forward(z)
        yield from ring_gather(lambda i: hg.at[i, :, c], z_ring, forward)
        yield
        arrive(forwards)

    def vocabulary():
        arrive(vx)
        in_v.wait()
        yield from ring_gather(lambda i: vg.at[i], z_ring, nothing)

    heads, vocabulary = heads(), vocabulary()
    step = lambda task: next(task, None)

    fwd = []
    for d, cp in zip(range(1, NX), tcp):
        cp.wait_recv()
        src = xo(NX - d)
        fwd.append(same(tk.at[c, src], partner))
    for cp in in_small:
        cp.wait()
    pick_rows = (iota((grp, nz * grp), 1) == iota((grp, nz * grp), 0) + z * grp).astype(BF16)
    own_routes = dot(pick_rows, routes_ref[...].astype(F32).astype(BF16), ((1,), (1,)))
    e0, e1 = own_routes[:, 0:1], own_routes[:, 1:2]
    row_t = iota((grp, 1), 0)
    block = (row_t >= TOK).astype(jnp.int32) + (row_t >= 2 * TOK).astype(jnp.int32) + (row_t >= 3 * TOK).astype(jnp.int32)
    col_t = iota((grp, grp), 1)
    lower = jnp.logical_and(col_t < row_t, col_t >= block * TOK).astype(F32).astype(BF16)
    lane_e = iota((grp, n_exp), 1).astype(F32)
    hot0, hot1 = (e0 == lane_e).astype(F32), (e1 == lane_e).astype(F32)
    earlier = dot(lower, (hot0 + hot1).astype(BF16))
    at_block = (block * CAP).astype(F32)
    place0 = e0 * ROWS + at_block + jnp.sum(hot0 * earlier, axis=1, keepdims=True)
    place1 = e1 * ROWS + at_block + jnp.sum(hot1 * earlier, axis=1, keepdims=True)
    own_slot = (iota((grp, ROWS), 1) + y * ROWS).astype(F32)
    select = ((place0 == own_slot).astype(F32) + (place1 == own_slot).astype(F32)).astype(BF16)
    arrive(fwd)
    square = jnp.zeros((grp, 1), F32)
    for h in range(2):
        rows = tk[h].astype(F32).reshape(grp, half)
        square = square + jnp.sum(rows * rows, axis=1, keepdims=True)
        for j in range(NX):
            tokf[h * NX + j] = rows[:, j * kcols : (j + 1) * kcols]
    scale = lax.rsqrt(square * (1.0 / d_model) + EPS)
    router = jnp.zeros((grp, n_exp), F32)
    for i in range(2 * NX):
        cols = slice(i * kcols, (i + 1) * kcols)
        normed = (tokf[i] * scale * ng_ref[:, cols]).astype(BF16)
        nbs[i] = normed
        router = router + dot(normed, wr_ref[:, cols], ((1,), (1,)))
    for j in range(NX):
        ag[c, z, j, NEAR] = dot(select[:, NEAR], nbs[c * NX + j], ((0,), (0,))).astype(BF16)
    ag[c, z, x, FAR] = dot(select[:, FAR], nbs[c * NX + x], ((0,), (0,))).astype(BF16)

    fwd = []
    forward = lambda ref: fwd.append(same(ref, partner))
    more = lambda: step(heads)
    gather(lambda i, j, rows: ag.at[c, i, j, rows], z_ring, forward, [more, nothing, more], skip_x=True)
    first = jax.nn.sigmoid(jnp.sum(router * (hot0 - hot1), axis=1, keepdims=True))
    lane_f = iota((grp, n_exp * ROWS), 1).astype(F32)
    weigh = first * (place0 == lane_f).astype(F32) + (1.0 - first) * (place1 == lane_f).astype(F32)
    weigh_hi = weigh.astype(BF16)
    weigh_lo = (weigh - weigh_hi.astype(F32)).astype(BF16)
    arrive(fwd)
    for cp in in_w:
        cp.wait()
    more()

    n_rows = nz * ROWS
    pre = jnp.zeros((n_rows, 256), F32)
    for h in range(2):
        for j in range(NX):
            i = h * NX + j
            pre = pre + dot(ag[h, :, j].reshape(n_rows, kcols), w_gu[i * kcols : (i + 1) * kcols, :])
    hidden = (jax.nn.silu(pre[:, :128]) * pre[:, 128:]).astype(BF16)

    def fill_rows(dst, core):
        w = wd.at[0 if core is c else 1]
        for j in range(NX):
            value = dot(hidden, w[:, j * kcols : (j + 1) * kcols])
            dst[:, j] = value.astype(dst.dtype).reshape(nz, ROWS, kcols)

    total = scatter(fill_rows, z_ring, dset, [more, more, lambda: (more(), step(vocabulary))])

    yg[y] = total.astype(BF16)
    across = two_step_gather(lambda i: yg.at[i], y_ring, lambda i: None)
    step(across)
    step(across)
    step(vocabulary)
    pump(across)
    outs = yg[...].reshape(n_exp * ROWS, kcols)
    mixed = tokf[c * NX + x] + dot(weigh_hi, outs) + dot(weigh_lo, outs)
    square = dot(jnp.ones((8, kcols), F32), mixed * mixed, ((1,), (1,)), HIGHEST)
    s1[:, 0:grp] = square[0:1, :]
    s1[:, grp:] = jnp.zeros((1, 128 - grp), F32)
    uq[c, x] = mixed.astype(BF16)
    ucp = [same(uq.at[c, x], peer) for peer in over_x]
    scp = [copy(s1, s2.at[x * 2 + c], peer) for peer in plane]
    fwd = [same(uq.at[c, x], partner)]
    step(heads)
    for d, cp in zip(range(1, NX), ucp):
        cp.wait_recv()
        fwd.append(same(uq.at[c, xo(NX - d)], partner))
    step(vocabulary)
    arrive(scp)
    square = s1[...]
    for a, b in near:
        square = square + s2[a * 2 + b]
    first_row = (iota((8, 128), 0) == 0).astype(F32)
    scale = lax.rsqrt(square * (1.0 / d_model) + EPS)
    scale = dot(jnp.broadcast_to(scale, (8, 128)), first_row, ((0,), (0,)), HIGHEST)[0:grp, 0:1]
    arrive(fwd)
    for h in range(2):
        for j in range(NX):
            i = h * NX + j
            cols = slice(i * kcols, (i + 1) * kcols)
            f96[:, cols] = (uq[h, j].astype(F32) * scale * fg_ref[:, cols]).astype(BF16)

    def window(z_):
        start = jnp.minimum(lax.div((z_ * NX + x) * vrow, 128) * 128, d_model - 256)
        return pl.ds(pl.multiple_of(start, 128), 256)

    tcp = [copy(f96.at[hrows(c), window(zo(d))], fw.at[z], peer) for d, peer in zip(range(1, nz), line_z)]
    fw[z] = f96[hrows(c), window(z)]
    ncp = copy(f96.at[0:16, :], fn, dev(z_=zo(-1)))

    pump(heads)
    preact = dot(f96[hrows(c), :], hg[...].reshape(d_model, kcols))
    sigma = jax.nn.sigmoid(preact)
    gfac[...] = sigma * (1.0 + preact * (1.0 - sigma))
    student = f96[hrows(c), ycols(y)].astype(F32) + preact * sigma
    sg[c, x, :, ycols(y)] = student.astype(BF16)

    fwd = []
    part = lambda i, j, rows: sg.at[c, j, rows, ALL if i is ALL else ycols(i)]
    gather(part, y_ring, forward_to(fwd, same, partner), [nothing, lambda: step(vocabulary)])
    pump(vocabulary)
    ncp.wait_recv()
    voc = vg[...].reshape(d_model, vcols)
    n_st = NX * grp
    ls[n_st : n_st + grp, :] = dot(f96[...], voc)
    ls[n_st + grp : n_st + grp + 16, :] = dot(fn[...], voc)
    ls[n_st + grp + 16 :, :] = jnp.zeros((16, vcols), F32)
    arrive(fwd)
    ls[0:n_st, :] = dot(sg[...].reshape(n_st, d_model), voc)

    def reduce_plane(src, first_in, second_in, result):
        cps = [copy(src, first_in.at[x * 2 + c], peer) for peer in plane]
        yield
        arrive(cps)
        row = src[...]
        for a, b in near:
            row = row + first_in[a * 2 + b]
        second_in[y] = row
        cps = [same(second_in.at[y], peer) for peer in line_y]
        yield
        arrive(cps)
        row = second_in[0]
        for i in range(1, ny):
            row = row + second_in[i]
        result.append(row)

    ones = jnp.ones((8, vcols), F32)
    sums[...] = dot(ones, jnp.exp(ls[...]), ((1,), (1,)), HIGHEST)[0:1, :]
    result = []
    pump(reduce_plane(sums, r1, r2, result))
    logs = jnp.log(result[0])
    n_all = ls.shape[0]
    column = dot(jnp.broadcast_to(logs, (8, n_all)), first_row, ((0,), (0,)), HIGHEST)[:, 0:1]
    tl[...] = ls[n_st : n_st + tl.shape[0], :] - column[n_st : n_st + tl.shape[0]]
    losses = [None] * NX
    row_id = iota((ROWS, 1), 0)
    n_tok = nz * grp
    for h in range(2):
        for k in range(NX):
            at = (h * NX + k) * ROWS
            logp = ls[at : at + ROWS, :] - column[at : at + ROWS]
            target = tl[h * ROWS + k + 1 : h * ROWS + k + 1 + ROWS, :]
            p = jnp.exp(target)
            weight = jnp.where(z * grp + h * ROWS + row_id + (k + 1) < n_tok, 1.0 / (n_tok - k - 1), 0.0)
            terms = jnp.sum(weight * (p * (target - logp)), axis=0, keepdims=True)
            losses[k] = terms if losses[k] is None else losses[k] + terms
            sl[h, k * ROWS : (k + 1) * ROWS, :] = (weight * (jnp.exp(logp) - p)).astype(BF16)
    for k in range(NX):
        lsum[:, k * 128 : (k + 1) * 128] = losses[k][:, :128] + losses[k][:, 128:]

    def fill_back(dst, core):
        for i in range(ny):
            value = dot(sl[core], vg[i], ((1,), (1,)))
            dst[i] = value.astype(dst.dtype).reshape(NX, ROWS, kcols)

    loss_rows = []

    def loss_task():
        result = []
        yield from reduce_plane(lsum, q1, q2, result)
        q3[z] = result[0]
        cps = [same(q3.at[z], peer) for peer in line_z]
        yield
        arrive(cps)
        row = q3[0]
        for i in range(1, nz):
            row = row + q3[i]
        loss_rows.append(row)

    def turn():
        arrive(tcp)
        lhs_t[...] = fw[...].reshape(nz * ROWS, 256).astype(F32).T.astype(BF16)

    task = loss_task()
    go_on = lambda: step(task)
    go_on()
    back = scatter(fill_back, y_ring, hset, [go_on, go_on])
    gg[z, x] = (back * gfac[...]).astype(BF16)

    gather(lambda i, j, rows: gg.at[i, j, rows], z_ring, None, [lambda: (turn(), go_on())])

    cut = dp * vrow - jnp.minimum(lax.div(dp * vrow, 128) * 128, d_model - 256)
    lhs = lhs_t[pl.ds(pl.multiple_of(cut, 32), vrow), :]
    cols = kcols // 2
    for k in range(NX):
        o = dot(lhs, gg[:, k].reshape(nz * ROWS, kcols))
        low, high = o[:, :cols], o[:, cols:]
        osd[k] = jnp.where(c == 0, high, low)
        out_ref[k] = jnp.where(c == 0, low, high)
    ocp = copy(osd, ord_, partner)
    row = loss_rows[0]
    for k in range(NX):
        loss_ref[k] = jnp.sum(row[:, k * 128 : (k + 1) * 128])
    ocp.wait_recv()
    out_ref[...] = out_ref[...] + ord_[...]
    for cp in sent:
        cp.wait_send()


def forward_to(forwards, same, partner):
    return lambda ref: forwards.append(same(ref, partner))


def solution(mesh):
    nz, ny = mesh.shape["dp"] // NX, mesh.shape["expert"] // 2

    def shards(tokens, routes, w_router, norm_gain, w_gate, w_up, w_down, final_gain, head_weights, vocab_proj):
        d_model = tokens.shape[1]
        half = d_model // 2
        kcols = d_model // ny
        vcols = vocab_proj.shape[1] // NX
        grp = NX * TOK
        vm = pltpu.VMEM

        def scatter_set(n, own):
            return (
                vm((n, NX, ROWS, kcols), own),
                vm((n, NX, ROWS, kcols), BF16),
                vm((n, NX, ROWS, kcols), BF16),
                vm((NX - 1, n, ROWS, kcols), BF16),
                vm((NX - 1, n, ROWS, kcols), BF16),
                vm((n, ROWS, kcols), BF16),
                vm((n, ROWS, kcols), BF16),
            )

        flat = [
            vm(tokens.shape, BF16),
            vm(routes.shape[::-1], jnp.int32),
            vm(w_router.shape[::-1], BF16),
            vm((1, d_model), F32),
            vm((1, d_model), F32),
            vm(head_weights.shape, BF16),
            vm((d_model, 256), BF16),
            vm((2, 128, half), BF16),
            vm((nz, d_model // nz, vcols), BF16),
            vm((NX, ROWS, kcols // 2), BF16),
            vm((NX, ROWS, kcols), BF16),
            vm((nz, NX, 2, ROWS, kcols), BF16),
            vm((2, NX, TOK, half), BF16),
            vm((2 * NX, grp, kcols), F32),
            vm((2 * NX, grp, kcols), BF16),
            vm((2, nz, NX, ROWS, kcols), BF16),
            vm((ny, ROWS, kcols), BF16),
            vm((2, NX, grp, kcols), BF16),
            vm((grp, d_model), BF16),
            vm((nz, ROWS, 256), BF16),
            vm((16, d_model), BF16),
            vm((ROWS, kcols), F32),
            vm((2, NX, ROWS, d_model), BF16),
            vm((512, vcols), F32),
            vm((grp + 16, vcols), F32),
            vm((1, 512), F32),
            vm((1, 512), F32),
            vm((2, NX * ROWS, vcols), BF16),
            vm((nz, NX, ROWS, kcols), BF16),
            vm((NX, 96, kcols // 2), F32),
            vm((NX, 96, kcols // 2), F32),
            vm((256, nz * ROWS), BF16),
            vm((1, 128), F32),
            vm((2 * NX, 1, 128), F32),
            vm((2 * NX, 1, 512), F32),
            vm((ny, 1, 512), F32),
            vm((2 * NX, 1, 512), F32),
            vm((ny, 1, 512), F32),
            vm((nz, 1, 512), F32),
        ]
        scratch = flat + [
            scatter_set(nz, F32),
            scatter_set(ny, F32),
            pltpu.SemaphoreType.DMA((N_COPIES,)),
            pltpu.SemaphoreType.DMA((N_COPIES,)),
            pltpu.SemaphoreType.DMA((16,)),
        ]

        def kernel(*refs):
            body(nz, ny, *refs)

        in_vmem = pl.BlockSpec(memory_space=pltpu.VMEM)
        in_hbm = pl.BlockSpec(memory_space=pl.ANY)
        losses, grads = pl.pallas_call(
            kernel,
            out_shape=(
                jax.ShapeDtypeStruct((NX,), F32),
                jax.ShapeDtypeStruct((NX, 96, kcols // 2), F32),
            ),
            in_specs=[in_hbm] * 10,
            out_specs=(pl.BlockSpec(memory_space=pltpu.SMEM), in_vmem),
            scratch_shapes=scratch,
            compiler_params=pltpu.CompilerParams(
                collective_id=0, has_side_effects=True, vmem_limit_bytes=60 * 2**20
            ),
            name="step",
        )(
            tokens,
            routes.T,
            w_router.T,
            norm_gain[None],
            final_gain[None],
            head_weights,
            w_gate[0],
            w_up[0],
            w_down[0],
            vocab_proj,
        )
        return losses, grads

    in_specs = (
        P("dp", None),
        P(),
        P(),
        P(),
        P("expert", None, "dp"),
        P("expert", None, "dp"),
        P("expert", "dp", None),
        P(),
        P(None, "dp", "expert"),
        P("dp", "expert"),
    )
    out_specs = (P(), P(None, "dp", "expert"))
    return jax.shard_map(shards, mesh=mesh, in_specs=in_specs, out_specs=out_specs, check_vma=False)
```

```python
import jax
import jax.numpy as jnp
from jax import lax
from jax.experimental import pallas as pl
from jax.experimental.pallas import tpu as pltpu
from jax.sharding import PartitionSpec as P

MESH = pl.DeviceIdType.MESH
F32, BF16 = jnp.float32, jnp.bfloat16
HIGHEST = lax.Precision.HIGHEST
EPS = 1e-05
NX = 4
TOK, CAP, SLOT = 24, 12, 16
N_COPIES = 480
ROWS = 48
ALL = slice(None)
NEAR, FAR = slice(0, 16), slice(16, 48)


def dot(a, b, dims=((1,), (0,)), precision=None):
    return lax.dot_general(a, b, (dims, ((), ())), precision=precision, preferred_element_type=F32)


def iota(shape, axis):
    return lax.broadcasted_iota(jnp.int32, shape, axis)


def pump(*tasks):
    live = list(tasks)
    while live:
        live = [task for task in live if next(task, live) is not live]


def body(
    nz, ny, tok_hbm, routes_hbm, wr_hbm, ng_hbm, fg_hbm, hw_hbm, wg_hbm, wu_hbm, wd_hbm, voc_hbm, loss_ref, out_ref,
    tok_ref, routes_ref, wr_ref, ng_ref, fg_ref, hw_ref, w_gu, wd, vg, hx, hl, hg, tk, tokf, nbs, ag, yg, uq, f96, fw, fn, gfac, sg,
    ls, tl, sums, lsum, sl, gg, osd, ord_, lhs_t, s1, s2, r1, r2, q1, q2, q3, dset, hset,
    ss, rs, lsem,
):
    dp, ex = lax.axis_index("dp"), lax.axis_index("expert")
    z, x = lax.div(dp, NX), lax.rem(dp, NX)
    y, c = lax.div(ex, 2), lax.rem(ex, 2)
    oc = 1 - c
    d_model = tok_ref.shape[1]
    half = d_model // 2
    vcols = vg.shape[2]
    kcols = d_model // ny
    grp = NX * TOK
    n_exp = wr_ref.shape[0]

    def dev(z_=None, x_=None, y_=None, c_=None):
        z_, x_ = (z if z_ is None else z_), (x if x_ is None else x_)
        y_, c_ = (y if y_ is None else y_), (c if c_ is None else c_)
        return {"dp": z_ * NX + x_, "expert": y_ * 2 + c_}

    def xo(d):
        return lax.rem(x + (d + NX), NX)

    def zo(d):
        return lax.rem(z + (d + nz), nz)

    def yo(d):
        return lax.rem(y + (d + ny), ny)

    partner = dev(c_=oc)
    over_x = [dev(x_=xo(d)) for d in range(1, NX)]
    sign = 1 - 2 * c
    z_ring = (nz, zo, lambda d: dev(z_=zo(d)))
    y_ring = (ny, yo, lambda d: dev(y_=yo(d)))
    sent = []

    def copy(src, dst, device):
        i = len(sent)
        cp = pltpu.make_async_remote_copy(
            src_ref=src, dst_ref=dst, send_sem=ss.at[i], recv_sem=rs.at[i], device_id=device, device_id_type=MESH
        )
        cp.start()
        sent.append(cp)
        return cp

    def same(ref, device):
        return copy(ref, ref, device)

    locals_ = []

    def local(src, dst):
        cp = pltpu.make_async_copy(src, dst, lsem.at[len(locals_)])
        cp.start()
        locals_.append(cp)
        return cp

    def arrive(copies):
        for cp in copies:
            cp.wait_recv()

    vrow = d_model // (nz * NX)
    quarter = lambda x_: pl.ds(pl.multiple_of(x_ * vcols, 128), vcols)
    hcols = lambda c_: pl.ds(pl.multiple_of(c_ * half, 128), half)
    ycols = lambda y_: pl.ds(pl.multiple_of(y_ * kcols, 128), kcols)
    vslot = lambda x_: pl.ds(pl.multiple_of(x_ * vrow, 16), vrow)
    in_tok = local(tok_hbm, tok_ref)
    in_small = [
        local(src, dst)
        for src, dst in (
            (routes_hbm, routes_ref),
            (wr_hbm, wr_ref),
            (ng_hbm, ng_ref),
            (fg_hbm, fg_ref),
            (hw_hbm, hw_ref),
        )
    ]
    in_w = [
        local(wg_hbm, w_gu.at[:, 0:128]),
        local(wu_hbm, w_gu.at[:, 128:256]),
        local(wd_hbm.at[:, hcols(c)], wd.at[0]),
        local(wd_hbm.at[:, hcols(oc)], wd.at[1]),
    ]
    in_v = local(voc_hbm.at[:, quarter(x)], vg.at[z, vslot(x), :])

    barrier = pltpu.get_barrier_semaphore()
    line_z = [dev(z_=zo(d)) for d in range(1, nz)]
    line_y = [dev(y_=yo(d)) for d in range(1, ny)]
    near = [(xo(d), c_) for d in range(1, NX) for c_ in (c, oc)] + [(x, oc)]
    plane = [dev(x_=a, c_=b) for a, b in near]
    peers = line_z + line_y + plane
    for peer in peers:
        pl.semaphore_signal(barrier, inc=1, device_id=peer, device_id_type=MESH)
    in_tok.wait()
    tk[c, x] = tok_ref[:, hcols(c)]
    tk[oc, x] = tok_ref[:, hcols(oc)]
    pl.semaphore_wait(barrier, len(peers))

    tcp = [copy(tok_ref.at[:, hcols(c)], tk.at[c, x], peer) for peer in over_x]

    def ring_gather(at, ring, on_arrival):
        n, off, to = ring
        h = n // 2
        a, b = same(at(off(0)), to(1)), same(at(off(0)), to(-1))
        for s in range(1, h + 1):
            yield
            a.wait_recv()
            if s < h:
                a = same(at(off(-s)), to(1))
            on_arrival(off(-s))
            if s < h:
                b.wait_recv()
                if s < h - 1:
                    b = same(at(off(s)), to(-1))
                on_arrival(off(s))

    def two_step_gather(at, ring, on_arrival):
        _, off, to = ring
        cps = {o: same(at(off(0)), to(o)) for o in (2, -2, 1, -1)}
        yield
        cps[2].wait_recv()
        cps[3] = same(at(off(-2)), to(1))
        cps[-2].wait_recv()
        cps[-3] = same(at(off(2)), to(-1))
        cps[4] = same(at(off(-2 * sign)), to(2 * sign))
        for o in (2, -2):
            on_arrival(off(-o))
        for o in (1, -1):
            cps[o].wait_recv()
            on_arrival(off(-o))
        yield
        for o in (3, -3, 4):
            cps[o].wait_recv()
            on_arrival(off(-o))

    def gather(at, ring, on_arrival=None, hooks=(), skip_x=False):
        _, off, to = ring
        take = on_arrival or (lambda ref: None)
        hooks = list(hooks)

        def hook():
            if hooks:
                hooks.pop(0)()

        on_x = []

        def over(o):
            ref = at(off(o), x, FAR)
            on_x.append((off(o), [same(ref, peer) for peer in over_x]))
            take(ref)

        bundle = lambda i: at(i, ALL, NEAR)
        near = two_step_gather(bundle, ring, lambda i: take(bundle(i)))
        cps = {o: same(at(off(0), x, FAR), to(o)) for o in (1, -1, 2, -2, 3, -3, 4)}
        if skip_x:
            take(bundle(off(0)))
            step(near)
        else:
            x_cps = [same(at(off(0), x, NEAR), peer) for peer in over_x]
        over(0)
        hook()
        for o, cp in cps.items():
            cp.wait_recv()
            over(-o)
            if o == -1 and not skip_x:
                arrive(x_cps)
                take(bundle(off(0)))
                step(near)
        hook()
        step(near)
        hook()
        for i, by_peer in on_x:
            for d, cp in zip(range(1, NX), by_peer):
                cp.wait_recv()
                take(at(i, xo(NX - d), FAR))
        hook()
        step(near)
        while hooks:
            hook()

    def scatter(fill, ring, bufs, hooks=()):
        po, ps, pr, x1s, x1r, zs, zr = bufs
        n, off, to = ring
        order = (4, 3, -3, 2, -2, 1, -1, 0)
        hooks = list(hooks)

        def hook():
            if hooks:
                hooks.pop(0)()

        got = {}
        for o in order:
            fill(ps, oc, o)
            got[o] = copy(ps.at[off(o)], pr.at[off(o)], partner)
        for o in order:
            fill(po, c, o)
        cps = {}
        way = {o: (1, -1)[k % 2] for k, o in enumerate(order)}

        def own(o, j):
            return po[off(o), j] + pr[off(o), j].astype(F32)

        def send(i, o, value, d):
            x1s[i, off(o)] = value.astype(BF16)
            cps[i, o] = copy(x1s.at[i, off(o)], x1r.at[i, off(o)], dev(x_=xo(d)))

        def out(o):
            got[o].wait_recv()
            send(0, o, own(o, xo(2)), way[o])
            send(1, o, own(o, xo(-way[o])), -way[o])

        def middle(o):
            cps[0, o].wait_recv()
            send(2, o, own(o, xo(way[o])) + x1r[0, off(o)].astype(F32), way[o])

        def term(o):
            value = own(o, x)
            for i in (1, 2):
                cps[i, o].wait_recv()
                value = value + x1r[i, off(o)].astype(F32)
            return value

        last = []

        def along(o):
            zs[o % n] = term(o).astype(BF16)
            last.append(copy(zs.at[o % n], zr.at[o % n], to(o)))

        for o in order[:4]:
            out(o)
        hook()
        for o, later in zip(order[:4], order[4:]):
            out(later)
            middle(o)
        hook()
        for o, later in zip(order[:4], order[4:]):
            along(o)
            middle(later)
        for o in order[4:-1]:
            along(o)
        value = term(0)
        hook()
        arrive(last)
        for o in order[:-1]:
            value = value + zr[o % n].astype(F32)
        while hooks:
            hook()
        return value

    nothing = lambda *_: None

    hrows = lambda c_: pl.ds(pl.multiple_of(c_ * ROWS, 16), ROWS)
    vx = [copy(voc_hbm.at[:, quarter(xo(d))], vg.at[z, vslot(x), :], peer) for d, peer in zip(range(1, NX), over_x)]
    ex_h = copy(hw_hbm.at[:, hrows(oc), :], hx, partner)

    def heads():
        ex_h.wait_recv()
        for k in range(NX):
            mine, theirs = hw_ref[k, hrows(c), :], hx[k]
            left = jnp.where(c == 0, mine, theirs)
            right = jnp.where(c == 0, theirs, mine)
            hl[k] = jnp.concatenate([left, right], axis=1)
        cps = [copy(hl.at[xo(d)], hg.at[z, x, c], peer) for d, peer in zip(range(1, NX), over_x)]
        hg[z, x, c] = hl[x]
        yield
        arrive(cps)
        forwards = []

        def forward(i):
            forwards.append(same(hg.at[i, :, c], partner))

        forward(z)
        yield from ring_gather(lambda i: hg.at[i, :, c], z_ring, forward)
        yield
        arrive(forwards)

    def vocabulary():
        arrive(vx)
        in_v.wait()
        yield from ring_gather(lambda i: vg.at[i], z_ring, nothing)

    heads, vocabulary = heads(), vocabulary()
    step = lambda task: next(task, None)

    for cp in in_small:
        cp.wait()
    pick_rows = (iota((grp, nz * grp), 1) == iota((grp, nz * grp), 0) + z * grp).astype(BF16)
    own_routes = dot(pick_rows, routes_ref[...].astype(F32).astype(BF16), ((1,), (1,)))
    e0, e1 = own_routes[:, 0:1], own_routes[:, 1:2]
    row_t = iota((grp, 1), 0)
    block = (row_t >= TOK).astype(jnp.int32) + (row_t >= 2 * TOK).astype(jnp.int32) + (row_t >= 3 * TOK).astype(jnp.int32)
    col_t = iota((grp, grp), 1)
    lower = jnp.logical_and(col_t < row_t, col_t >= block * TOK).astype(F32).astype(BF16)
    lane_e = iota((grp, n_exp), 1).astype(F32)
    hot0, hot1 = (e0 == lane_e).astype(F32), (e1 == lane_e).astype(F32)
    earlier = dot(lower, (hot0 + hot1).astype(BF16))
    at_block = (block * CAP).astype(F32)
    place0 = e0 * ROWS + at_block + jnp.sum(hot0 * earlier, axis=1, keepdims=True)
    place1 = e1 * ROWS + at_block + jnp.sum(hot1 * earlier, axis=1, keepdims=True)
    own_slot = (iota((grp, ROWS), 1) + y * ROWS).astype(F32)
    select = ((place0 == own_slot).astype(F32) + (place1 == own_slot).astype(F32)).astype(BF16)
    fwd = []
    for d, cp in zip(range(1, NX), tcp):
        cp.wait_recv()
        src = xo(NX - d)
        fwd.append(same(tk.at[c, src], partner))
    arrive(fwd)
    square = jnp.zeros((grp, 1), F32)
    for h in range(2):
        rows = tk[h].astype(F32).reshape(grp, half)
        square = square + jnp.sum(rows * rows, axis=1, keepdims=True)
        for j in range(NX):
            tokf[h * NX + j] = rows[:, j * kcols : (j + 1) * kcols]
    scale = lax.rsqrt(square * (1.0 / d_model) + EPS)
    router = jnp.zeros((grp, n_exp), F32)
    for i in range(2 * NX):
        cols = slice(i * kcols, (i + 1) * kcols)
        normed = (tokf[i] * scale * ng_ref[:, cols]).astype(BF16)
        nbs[i] = normed
        router = router + dot(normed, wr_ref[:, cols], ((1,), (1,)))
    for j in range(NX):
        ag[c, z, j, NEAR] = dot(select[:, NEAR], nbs[c * NX + j], ((0,), (0,))).astype(BF16)
    ag[c, z, x, FAR] = dot(select[:, FAR], nbs[c * NX + x], ((0,), (0,))).astype(BF16)

    fwd = []
    forward = lambda ref: fwd.append(same(ref, partner))
    more = lambda: step(heads)
    gather(lambda i, j, rows: ag.at[c, i, j, rows], z_ring, forward, [more, nothing, more], skip_x=True)
    first = jax.nn.sigmoid(jnp.sum(router * (hot0 - hot1), axis=1, keepdims=True))
    lane_f = iota((grp, n_exp * ROWS), 1).astype(F32)
    weigh = first * (place0 == lane_f).astype(F32) + (1.0 - first) * (place1 == lane_f).astype(F32)
    weigh_hi = weigh.astype(BF16)
    weigh_lo = (weigh - weigh_hi.astype(F32)).astype(BF16)
    arrive(fwd)
    for cp in in_w:
        cp.wait()
    more()

    n_rows = nz * ROWS
    pre = jnp.zeros((n_rows, 256), F32)
    for h in range(2):
        for j in range(NX):
            i = h * NX + j
            pre = pre + dot(ag[h, :, j].reshape(n_rows, kcols), w_gu[i * kcols : (i + 1) * kcols, :])
    hidden = (jax.nn.silu(pre[:, :128]) * pre[:, 128:]).astype(BF16)

    def fill_rows(dst, core, o):
        if o != 4:
            return
        w = wd.at[0 if core is c else 1]
        for j in range(NX):
            value = dot(hidden, w[:, j * kcols : (j + 1) * kcols])
            dst[:, j] = value.astype(dst.dtype).reshape(nz, ROWS, kcols)

    total = scatter(fill_rows, z_ring, dset, [nothing, more, lambda: step(vocabulary)])

    yg[y] = total.astype(BF16)
    ycp = [same(yg.at[y], peer) for peer in line_y]
    more()
    arrive(ycp)
    more()
    step(vocabulary)
    outs = yg[...].reshape(n_exp * ROWS, kcols)
    mixed = tokf[c * NX + x] + dot(weigh_hi, outs) + dot(weigh_lo, outs)
    square = dot(jnp.ones((8, kcols), F32), mixed * mixed, ((1,), (1,)), HIGHEST)
    s1[:, 0:grp] = square[0:1, :]
    s1[:, grp:] = jnp.zeros((1, 128 - grp), F32)
    uq[c, x] = mixed.astype(BF16)
    ucp = [same(uq.at[c, x], peer) for peer in over_x]
    scp = [copy(s1, s2.at[x * 2 + c], peer) for peer in plane]
    fwd = [same(uq.at[c, x], partner)]
    step(heads)
    for d, cp in zip(range(1, NX), ucp):
        cp.wait_recv()
        fwd.append(same(uq.at[c, xo(NX - d)], partner))
    step(vocabulary)
    arrive(scp)
    square = s1[...]
    for a, b in near:
        square = square + s2[a * 2 + b]
    first_row = (iota((8, 128), 0) == 0).astype(F32)
    scale = lax.rsqrt(square * (1.0 / d_model) + EPS)
    scale = dot(jnp.broadcast_to(scale, (8, 128)), first_row, ((0,), (0,)), HIGHEST)[0:grp, 0:1]
    arrive(fwd)
    for h in range(2):
        for j in range(NX):
            i = h * NX + j
            cols = slice(i * kcols, (i + 1) * kcols)
            f96[:, cols] = (uq[h, j].astype(F32) * scale * fg_ref[:, cols]).astype(BF16)

    def window(z_):
        start = jnp.minimum(lax.div((z_ * NX + x) * vrow, 128) * 128, d_model - 256)
        return pl.ds(pl.multiple_of(start, 128), 256)

    tcp = [copy(f96.at[hrows(c), window(zo(d))], fw.at[z], peer) for d, peer in zip(range(1, nz), line_z)]
    fw[z] = f96[hrows(c), window(z)]
    ncp = copy(f96.at[0:16, :], fn, dev(z_=zo(-1)))

    pump(heads)
    preact = dot(f96[hrows(c), :], hg[...].reshape(d_model, kcols))
    sigma = jax.nn.sigmoid(preact)
    gfac[...] = sigma * (1.0 + preact * (1.0 - sigma))
    student = f96[hrows(c), ycols(y)].astype(F32) + preact * sigma
    sg[c, x, :, ycols(y)] = student.astype(BF16)

    fwd = []
    part = lambda i, j, rows: sg.at[c, j, rows, ALL if i is ALL else ycols(i)]
    gather(part, y_ring, forward_to(fwd, same, partner), [nothing, lambda: step(vocabulary)])
    pump(vocabulary)
    ncp.wait_recv()
    voc = vg[...].reshape(d_model, vcols)
    n_st = NX * grp
    ls[n_st : n_st + grp, :] = dot(f96[...], voc)
    ls[n_st + grp : n_st + grp + 16, :] = dot(fn[...], voc)
    ls[n_st + grp + 16 :, :] = jnp.zeros((16, vcols), F32)
    arrive(fwd)
    ls[0:n_st, :] = dot(sg[...].reshape(n_st, d_model), voc)

    def reduce_plane(src, first_in, second_in, result):
        cps = [copy(src, first_in.at[x * 2 + c], peer) for peer in plane]
        yield
        arrive(cps)
        row = src[...]
        for a, b in near:
            row = row + first_in[a * 2 + b]
        second_in[y] = row
        cps = [same(second_in.at[y], peer) for peer in line_y]
        yield
        arrive(cps)
        row = second_in[0]
        for i in range(1, ny):
            row = row + second_in[i]
        result.append(row)

    ones = jnp.ones((8, vcols), F32)
    sums[...] = dot(ones, jnp.exp(ls[...]), ((1,), (1,)), HIGHEST)[0:1, :]
    result = []
    pump(reduce_plane(sums, r1, r2, result))
    logs = jnp.log(result[0])
    n_all = ls.shape[0]
    column = dot(jnp.broadcast_to(logs, (8, n_all)), first_row, ((0,), (0,)), HIGHEST)[:, 0:1]
    tl[...] = ls[n_st : n_st + tl.shape[0], :] - column[n_st : n_st + tl.shape[0]]
    losses = [None] * NX
    row_id = iota((ROWS, 1), 0)
    n_tok = nz * grp
    for h in range(2):
        for k in range(NX):
            at = (h * NX + k) * ROWS
            logp = ls[at : at + ROWS, :] - column[at : at + ROWS]
            target = tl[h * ROWS + k + 1 : h * ROWS + k + 1 + ROWS, :]
            p = jnp.exp(target)
            weight = jnp.where(z * grp + h * ROWS + row_id + (k + 1) < n_tok, 1.0 / (n_tok - k - 1), 0.0)
            terms = jnp.sum(weight * (p * (target - logp)), axis=0, keepdims=True)
            losses[k] = terms if losses[k] is None else losses[k] + terms
            sl[h, k * ROWS : (k + 1) * ROWS, :] = (weight * (jnp.exp(logp) - p)).astype(BF16)
    for k in range(NX):
        lsum[:, k * 128 : (k + 1) * 128] = losses[k][:, :128] + losses[k][:, 128:]

    def fill_back(dst, core, o):
        value = dot(sl[core], vg[yo(o)], ((1,), (1,)))
        dst[yo(o)] = value.astype(dst.dtype).reshape(NX, ROWS, kcols)

    loss_rows = []

    def loss_task():
        result = []
        yield from reduce_plane(lsum, q1, q2, result)
        q3[z] = result[0]
        cps = [same(q3.at[z], peer) for peer in line_z]
        yield
        arrive(cps)
        row = q3[0]
        for i in range(1, nz):
            row = row + q3[i]
        loss_rows.append(row)

    def turn():
        arrive(tcp)
        lhs_t[...] = fw[...].reshape(nz * ROWS, 256).astype(F32).T.astype(BF16)

    task = loss_task()
    go_on = lambda: step(task)
    go_on()
    back = scatter(fill_back, y_ring, hset, [go_on, go_on])
    gg[z, x] = (back * gfac[...]).astype(BF16)

    gather(lambda i, j, rows: gg.at[i, j, rows], z_ring, None, [lambda: (turn(), go_on())])

    cut = dp * vrow - jnp.minimum(lax.div(dp * vrow, 128) * 128, d_model - 256)
    lhs = lhs_t[pl.ds(pl.multiple_of(cut, 32), vrow), :]
    cols = kcols // 2
    for k in range(NX):
        o = dot(lhs, gg[:, k].reshape(nz * ROWS, kcols))
        low, high = o[:, :cols], o[:, cols:]
        osd[k] = jnp.where(c == 0, high, low).astype(BF16)
        out_ref[k] = jnp.where(c == 0, low, high)
    ocp = copy(osd, ord_, partner)
    row = loss_rows[0]
    for k in range(NX):
        loss_ref[k] = jnp.sum(row[:, k * 128 : (k + 1) * 128])
    ocp.wait_recv()
    out_ref[...] = out_ref[...] + ord_[...].astype(F32)
    for cp in sent:
        cp.wait_send()


def forward_to(forwards, same, partner):
    return lambda ref: forwards.append(same(ref, partner))


def solution(mesh):
    nz, ny = mesh.shape["dp"] // NX, mesh.shape["expert"] // 2

    def shards(tokens, routes, w_router, norm_gain, w_gate, w_up, w_down, final_gain, head_weights, vocab_proj):
        d_model = tokens.shape[1]
        half = d_model // 2
        kcols = d_model // ny
        vcols = vocab_proj.shape[1] // NX
        grp = NX * TOK
        vm = pltpu.VMEM

        def scatter_set(n, own):
            return (
                vm((n, NX, ROWS, kcols), own),
                vm((n, NX, ROWS, kcols), BF16),
                vm((n, NX, ROWS, kcols), BF16),
                vm((NX - 1, n, ROWS, kcols), BF16),
                vm((NX - 1, n, ROWS, kcols), BF16),
                vm((n, ROWS, kcols), BF16),
                vm((n, ROWS, kcols), BF16),
            )

        flat = [
            vm(tokens.shape, BF16),
            vm(routes.shape[::-1], jnp.int32),
            vm(w_router.shape[::-1], BF16),
            vm((1, d_model), F32),
            vm((1, d_model), F32),
            vm(head_weights.shape, BF16),
            vm((d_model, 256), BF16),
            vm((2, 128, half), BF16),
            vm((nz, d_model // nz, vcols), BF16),
            vm((NX, ROWS, kcols // 2), BF16),
            vm((NX, ROWS, kcols), BF16),
            vm((nz, NX, 2, ROWS, kcols), BF16),
            vm((2, NX, TOK, half), BF16),
            vm((2 * NX, grp, kcols), F32),
            vm((2 * NX, grp, kcols), BF16),
            vm((2, nz, NX, ROWS, kcols), BF16),
            vm((ny, ROWS, kcols), BF16),
            vm((2, NX, grp, kcols), BF16),
            vm((grp, d_model), BF16),
            vm((nz, ROWS, 256), BF16),
            vm((16, d_model), BF16),
            vm((ROWS, kcols), F32),
            vm((2, NX, ROWS, d_model), BF16),
            vm((512, vcols), F32),
            vm((grp + 16, vcols), F32),
            vm((1, 512), F32),
            vm((1, 512), F32),
            vm((2, NX * ROWS, vcols), BF16),
            vm((nz, NX, ROWS, kcols), BF16),
            vm((NX, 96, kcols // 2), BF16),
            vm((NX, 96, kcols // 2), BF16),
            vm((256, nz * ROWS), BF16),
            vm((1, 128), F32),
            vm((2 * NX, 1, 128), F32),
            vm((2 * NX, 1, 512), F32),
            vm((ny, 1, 512), F32),
            vm((2 * NX, 1, 512), F32),
            vm((ny, 1, 512), F32),
            vm((nz, 1, 512), F32),
        ]
        scratch = flat + [
            scatter_set(nz, F32),
            scatter_set(ny, F32),
            pltpu.SemaphoreType.DMA((N_COPIES,)),
            pltpu.SemaphoreType.DMA((N_COPIES,)),
            pltpu.SemaphoreType.DMA((16,)),
        ]

        def kernel(*refs):
            body(nz, ny, *refs)

        in_vmem = pl.BlockSpec(memory_space=pltpu.VMEM)
        in_hbm = pl.BlockSpec(memory_space=pl.ANY)
        losses, grads = pl.pallas_call(
            kernel,
            out_shape=(
                jax.ShapeDtypeStruct((NX,), F32),
                jax.ShapeDtypeStruct((NX, 96, kcols // 2), F32),
            ),
            in_specs=[in_hbm] * 10,
            out_specs=(pl.BlockSpec(memory_space=pltpu.SMEM), in_vmem),
            scratch_shapes=scratch,
            compiler_params=pltpu.CompilerParams(
                collective_id=0, has_side_effects=True, vmem_limit_bytes=60 * 2**20
            ),
            name="step",
        )(
            tokens,
            routes.T,
            w_router.T,
            norm_gain[None],
            final_gain[None],
            head_weights,
            w_gate[0],
            w_up[0],
            w_down[0],
            vocab_proj,
        )
        return losses, grads

    in_specs = (
        P("dp", None),
        P(),
        P(),
        P(),
        P("expert", None, "dp"),
        P("expert", None, "dp"),
        P("expert", "dp", None),
        P(),
        P(None, "dp", "expert"),
        P("dp", "expert"),
    )
    out_specs = (P(), P(None, "dp", "expert"))
    return jax.shard_map(shards, mesh=mesh, in_specs=in_specs, out_specs=out_specs, check_vma=False)
```

```python
import jax
import jax.numpy as jnp
from jax import lax
from jax.experimental import pallas as pl
from jax.experimental.pallas import tpu as pltpu
from jax.sharding import PartitionSpec as P

MESH = pl.DeviceIdType.MESH
F32, BF16 = jnp.float32, jnp.bfloat16
HIGHEST = lax.Precision.HIGHEST
EPS = 1e-05
NX = 4
TOK, CAP, SLOT = 24, 12, 16
N_COPIES = 480
ROWS = 48
ALL = slice(None)
NEAR, FAR = slice(0, 16), slice(16, 48)


def dot(a, b, dims=((1,), (0,)), precision=None):
    return lax.dot_general(a, b, (dims, ((), ())), precision=precision, preferred_element_type=F32)


def iota(shape, axis):
    return lax.broadcasted_iota(jnp.int32, shape, axis)


def pump(*tasks):
    live = list(tasks)
    while live:
        live = [task for task in live if next(task, live) is not live]


def body(
    nz, ny, tok_hbm, routes_hbm, wr_hbm, ng_hbm, fg_hbm, hw_hbm, wg_hbm, wu_hbm, wd_hbm, voc_hbm, loss_ref, out_ref,
    tok_ref, routes_ref, wr_ref, ng_ref, fg_ref, hw_ref, w_gu, wd, vg, hx, hl, hg, tk, tokf, nbs, ag, yg, uq, f96, fw, fn, gfac, sg,
    ls, tl, sums, lsum, sl, gg, osd, ord_, lhs_t, s1, s2, r1, r2, q1, q2, q3, dset, hset,
    ss, rs, lsem,
):
    dp, ex = lax.axis_index("dp"), lax.axis_index("expert")
    z, x = lax.div(dp, NX), lax.rem(dp, NX)
    y, c = lax.div(ex, 2), lax.rem(ex, 2)
    oc = 1 - c
    d_model = tok_ref.shape[1]
    half = d_model // 2
    vcols = vg.shape[2]
    kcols = d_model // ny
    grp = NX * TOK
    n_exp = wr_ref.shape[0]

    def dev(z_=None, x_=None, y_=None, c_=None):
        z_, x_ = (z if z_ is None else z_), (x if x_ is None else x_)
        y_, c_ = (y if y_ is None else y_), (c if c_ is None else c_)
        return {"dp": z_ * NX + x_, "expert": y_ * 2 + c_}

    def xo(d):
        return lax.rem(x + (d + NX), NX)

    def zo(d):
        return lax.rem(z + (d + nz), nz)

    def yo(d):
        return lax.rem(y + (d + ny), ny)

    partner = dev(c_=oc)
    over_x = [dev(x_=xo(d)) for d in range(1, NX)]
    sign = 1 - 2 * c
    z_ring = (nz, zo, lambda d: dev(z_=zo(d)))
    y_ring = (ny, yo, lambda d: dev(y_=yo(d)))
    sent = []

    def copy(src, dst, device):
        i = len(sent)
        cp = pltpu.make_async_remote_copy(
            src_ref=src, dst_ref=dst, send_sem=ss.at[i], recv_sem=rs.at[i], device_id=device, device_id_type=MESH
        )
        cp.start()
        sent.append(cp)
        return cp

    def same(ref, device):
        return copy(ref, ref, device)

    locals_ = []

    def local(src, dst):
        cp = pltpu.make_async_copy(src, dst, lsem.at[len(locals_)])
        cp.start()
        locals_.append(cp)
        return cp

    def arrive(copies):
        for cp in copies:
            cp.wait_recv()

    vrow = d_model // (nz * NX)
    quarter = lambda x_: pl.ds(pl.multiple_of(x_ * vcols, 128), vcols)
    hcols = lambda c_: pl.ds(pl.multiple_of(c_ * half, 128), half)
    ycols = lambda y_: pl.ds(pl.multiple_of(y_ * kcols, 128), kcols)
    vslot = lambda x_: pl.ds(pl.multiple_of(x_ * vrow, 16), vrow)
    in_tok = local(tok_hbm, tok_ref)
    in_small = [
        local(src, dst)
        for src, dst in (
            (routes_hbm, routes_ref),
            (wr_hbm, wr_ref),
            (ng_hbm, ng_ref),
            (fg_hbm, fg_ref),
            (hw_hbm, hw_ref),
        )
    ]
    in_w = [
        local(wg_hbm, w_gu.at[:, 0:128]),
        local(wu_hbm, w_gu.at[:, 128:256]),
        local(wd_hbm.at[:, hcols(c)], wd.at[0]),
        local(wd_hbm.at[:, hcols(oc)], wd.at[1]),
    ]
    in_v = local(voc_hbm.at[:, quarter(x)], vg.at[z, vslot(x), :])

    barrier = pltpu.get_barrier_semaphore()
    line_z = [dev(z_=zo(d)) for d in range(1, nz)]
    line_y = [dev(y_=yo(d)) for d in range(1, ny)]
    near = [(xo(d), c_) for d in range(1, NX) for c_ in (c, oc)] + [(x, oc)]
    plane = [dev(x_=a, c_=b) for a, b in near]
    peers = line_z + line_y + plane
    for peer in peers:
        pl.semaphore_signal(barrier, inc=1, device_id=peer, device_id_type=MESH)
    in_tok.wait()
    tk[c, x] = tok_ref[:, hcols(c)]
    tk[oc, x] = tok_ref[:, hcols(oc)]
    pl.semaphore_wait(barrier, len(peers))

    tcp = [copy(tok_ref.at[:, hcols(c)], tk.at[c, x], peer) for peer in over_x]

    def ring_gather(at, ring, on_arrival):
        n, off, to = ring
        h = n // 2
        a, b = same(at(off(0)), to(1)), same(at(off(0)), to(-1))
        for s in range(1, h + 1):
            yield
            a.wait_recv()
            if s < h:
                a = same(at(off(-s)), to(1))
            on_arrival(off(-s))
            if s < h:
                b.wait_recv()
                if s < h - 1:
                    b = same(at(off(s)), to(-1))
                on_arrival(off(s))

    def two_step_gather(at, ring, on_arrival):
        _, off, to = ring
        cps = {o: same(at(off(0)), to(o)) for o in (2, -2, 1, -1)}
        yield
        cps[2].wait_recv()
        cps[3] = same(at(off(-2)), to(1))
        cps[-2].wait_recv()
        cps[-3] = same(at(off(2)), to(-1))
        cps[4] = same(at(off(-2 * sign)), to(2 * sign))
        for o in (2, -2):
            on_arrival(off(-o))
        for o in (1, -1):
            cps[o].wait_recv()
            on_arrival(off(-o))
        yield
        for o in (3, -3, 4):
            cps[o].wait_recv()
            on_arrival(off(-o))

    def gather(at, ring, on_arrival=None, hooks=(), skip_x=False):
        _, off, to = ring
        take = on_arrival or (lambda ref: None)
        hooks = list(hooks)

        def hook():
            if hooks:
                hooks.pop(0)()

        on_x = []

        def over(o):
            ref = at(off(o), x, FAR)
            on_x.append((off(o), [same(ref, peer) for peer in over_x]))
            take(ref)

        bundle = lambda i: at(i, ALL, NEAR)
        near = two_step_gather(bundle, ring, lambda i: take(bundle(i)))
        cps = {o: same(at(off(0), x, FAR), to(o)) for o in (1, -1, 2, -2, 3, -3, 4)}
        if skip_x:
            take(bundle(off(0)))
            step(near)
        else:
            x_cps = [same(at(off(0), x, NEAR), peer) for peer in over_x]
        over(0)
        hook()
        for o, cp in cps.items():
            cp.wait_recv()
            over(-o)
            if o == -1 and not skip_x:
                arrive(x_cps)
                take(bundle(off(0)))
                step(near)
        hook()
        step(near)
        hook()
        for i, by_peer in on_x:
            for d, cp in zip(range(1, NX), by_peer):
                cp.wait_recv()
                take(at(i, xo(NX - d), FAR))
        hook()
        step(near)
        while hooks:
            hook()

    def scatter(fill, ring, bufs, hooks=()):
        po, ps, pr, x1s, x1r, zs, zr = bufs
        n, off, to = ring
        order = (4, 3, -3, 2, -2, 1, -1, 0)
        hooks = list(hooks)

        def hook():
            if hooks:
                hooks.pop(0)()

        got = {}
        for o in order:
            fill(ps, oc, o)
            got[o] = copy(ps.at[off(o)], pr.at[off(o)], partner)
        for o in order:
            fill(po, c, o)
        cps = {}
        way = {o: (1, -1)[k % 2] for k, o in enumerate(order)}

        def own(o, j):
            return po[off(o), j] + pr[off(o), j].astype(F32)

        def send(i, o, value, d):
            x1s[i, off(o)] = value.astype(BF16)
            cps[i, o] = copy(x1s.at[i, off(o)], x1r.at[i, off(o)], dev(x_=xo(d)))

        def out(o):
            got[o].wait_recv()
            send(0, o, own(o, xo(2)), way[o])
            send(1, o, own(o, xo(-way[o])), -way[o])

        def middle(o):
            cps[0, o].wait_recv()
            send(2, o, own(o, xo(way[o])) + x1r[0, off(o)].astype(F32), way[o])

        def term(o):
            value = own(o, x)
            for i in (1, 2):
                cps[i, o].wait_recv()
                value = value + x1r[i, off(o)].astype(F32)
            return value

        last = []

        def along(o):
            zs[o % n] = term(o).astype(BF16)
            last.append(copy(zs.at[o % n], zr.at[o % n], to(o)))

        for o in order[:4]:
            out(o)
        hook()
        for o, later in zip(order[:4], order[4:]):
            out(later)
            middle(o)
        hook()
        for o, later in zip(order[:4], order[4:]):
            along(o)
            middle(later)
        for o in order[4:-1]:
            along(o)
        value = term(0)
        hook()
        arrive(last)
        for o in order[:-1]:
            value = value + zr[o % n].astype(F32)
        while hooks:
            hook()
        return value

    nothing = lambda *_: None

    hrows = lambda c_: pl.ds(pl.multiple_of(c_ * ROWS, 16), ROWS)
    vx = [copy(voc_hbm.at[:, quarter(xo(d))], vg.at[z, vslot(x), :], peer) for d, peer in zip(range(1, NX), over_x)]
    ex_h = copy(hw_hbm.at[:, hrows(oc), :], hx, partner)

    def heads():
        ex_h.wait_recv()
        for k in range(NX):
            mine, theirs = hw_ref[k, hrows(c), :], hx[k]
            left = jnp.where(c == 0, mine, theirs)
            right = jnp.where(c == 0, theirs, mine)
            hl[k] = jnp.concatenate([left, right], axis=1)
        cps = [copy(hl.at[xo(d)], hg.at[z, x, c], peer) for d, peer in zip(range(1, NX), over_x)]
        hg[z, x, c] = hl[x]
        yield
        arrive(cps)
        forwards = []

        def forward(i):
            forwards.append(same(hg.at[i, :, c], partner))

        forward(z)
        yield from ring_gather(lambda i: hg.at[i, :, c], z_ring, forward)
        yield
        arrive(forwards)

    def vocabulary():
        arrive(vx)
        in_v.wait()
        yield from ring_gather(lambda i: vg.at[i], z_ring, nothing)

    heads, vocabulary = heads(), vocabulary()
    step = lambda task: next(task, None)

    for cp in in_small:
        cp.wait()
    pick_rows = (iota((grp, nz * grp), 1) == iota((grp, nz * grp), 0) + z * grp).astype(BF16)
    own_routes = dot(pick_rows, routes_ref[...].astype(F32).astype(BF16), ((1,), (1,)))
    e0, e1 = own_routes[:, 0:1], own_routes[:, 1:2]
    row_t = iota((grp, 1), 0)
    block = (row_t >= TOK).astype(jnp.int32) + (row_t >= 2 * TOK).astype(jnp.int32) + (row_t >= 3 * TOK).astype(jnp.int32)
    col_t = iota((grp, grp), 1)
    lower = jnp.logical_and(col_t < row_t, col_t >= block * TOK).astype(F32).astype(BF16)
    lane_e = iota((grp, n_exp), 1).astype(F32)
    hot0, hot1 = (e0 == lane_e).astype(F32), (e1 == lane_e).astype(F32)
    earlier = dot(lower, (hot0 + hot1).astype(BF16))
    at_block = (block * CAP).astype(F32)
    place0 = e0 * ROWS + at_block + jnp.sum(hot0 * earlier, axis=1, keepdims=True)
    place1 = e1 * ROWS + at_block + jnp.sum(hot1 * earlier, axis=1, keepdims=True)
    own_slot = (iota((grp, ROWS), 1) + y * ROWS).astype(F32)
    select = ((place0 == own_slot).astype(F32) + (place1 == own_slot).astype(F32)).astype(BF16)
    fwd = []
    for d, cp in zip(range(1, NX), tcp):
        cp.wait_recv()
        src = xo(NX - d)
        fwd.append(same(tk.at[c, src], partner))
    arrive(fwd)
    square = jnp.zeros((grp, 1), F32)
    for h in range(2):
        rows = tk[h].astype(F32).reshape(grp, half)
        square = square + jnp.sum(rows * rows, axis=1, keepdims=True)
        for j in range(NX):
            tokf[h * NX + j] = rows[:, j * kcols : (j + 1) * kcols]
    scale = lax.rsqrt(square * (1.0 / d_model) + EPS)
    router = jnp.zeros((grp, n_exp), F32)
    for i in range(2 * NX):
        cols = slice(i * kcols, (i + 1) * kcols)
        normed = (tokf[i] * scale * ng_ref[:, cols]).astype(BF16)
        nbs[i] = normed
        router = router + dot(normed, wr_ref[:, cols], ((1,), (1,)))
    for j in range(NX):
        ag[c, z, j, NEAR] = dot(select[:, NEAR], nbs[c * NX + j], ((0,), (0,))).astype(BF16)
    ag[c, z, x, FAR] = dot(select[:, FAR], nbs[c * NX + x], ((0,), (0,))).astype(BF16)

    fwd = []
    forward = lambda ref: fwd.append(same(ref, partner))
    more = lambda: step(heads)
    gather(lambda i, j, rows: ag.at[c, i, j, rows], z_ring, forward, [more, nothing, more], skip_x=True)
    first = jax.nn.sigmoid(jnp.sum(router * (hot0 - hot1), axis=1, keepdims=True))
    lane_f = iota((grp, n_exp * ROWS), 1).astype(F32)
    weigh = first * (place0 == lane_f).astype(F32) + (1.0 - first) * (place1 == lane_f).astype(F32)
    weigh_hi = weigh.astype(BF16)
    weigh_lo = (weigh - weigh_hi.astype(F32)).astype(BF16)
    arrive(fwd)
    for cp in in_w:
        cp.wait()
    more()

    n_rows = nz * ROWS
    pre = jnp.zeros((n_rows, 256), F32)
    for h in range(2):
        for j in range(NX):
            i = h * NX + j
            pre = pre + dot(ag[h, :, j].reshape(n_rows, kcols), w_gu[i * kcols : (i + 1) * kcols, :])
    hidden = (jax.nn.silu(pre[:, :128]) * pre[:, 128:]).astype(BF16)

    def fill_rows(dst, core, o):
        if o != 4:
            return
        w = wd.at[0 if core is c else 1]
        for j in range(NX):
            value = dot(hidden, w[:, j * kcols : (j + 1) * kcols])
            dst[:, j] = value.astype(dst.dtype).reshape(nz, ROWS, kcols)

    total = scatter(fill_rows, z_ring, dset, [nothing, more, lambda: step(vocabulary)])

    yg[y] = total.astype(BF16)
    ycp = [same(yg.at[y], peer) for peer in line_y]
    more()
    arrive(ycp)
    more()
    step(vocabulary)
    outs = yg[...].reshape(n_exp * ROWS, kcols)
    mixed = tokf[c * NX + x] + dot(weigh_hi, outs) + dot(weigh_lo, outs)
    square = dot(jnp.ones((8, kcols), F32), mixed * mixed, ((1,), (1,)), HIGHEST)
    s1[:, 0:grp] = square[0:1, :]
    s1[:, grp:] = jnp.zeros((1, 128 - grp), F32)
    uq[c, x] = mixed.astype(BF16)
    ucp = [same(uq.at[c, x], peer) for peer in over_x]
    scp = [copy(s1, s2.at[x * 2 + c], peer) for peer in plane]
    fwd = [same(uq.at[c, x], partner)]
    step(heads)
    for d, cp in zip(range(1, NX), ucp):
        cp.wait_recv()
        fwd.append(same(uq.at[c, xo(NX - d)], partner))
    arrive(scp)
    square = s1[...]
    for a, b in near:
        square = square + s2[a * 2 + b]
    first_row = (iota((8, 128), 0) == 0).astype(F32)
    scale = lax.rsqrt(square * (1.0 / d_model) + EPS)
    scale = dot(jnp.broadcast_to(scale, (8, 128)), first_row, ((0,), (0,)), HIGHEST)[0:grp, 0:1]
    arrive(fwd)
    for h in range(2):
        for j in range(NX):
            i = h * NX + j
            cols = slice(i * kcols, (i + 1) * kcols)
            f96[:, cols] = (uq[h, j].astype(F32) * scale * fg_ref[:, cols]).astype(BF16)

    def window(z_):
        start = jnp.minimum(lax.div((z_ * NX + x) * vrow, 128) * 128, d_model - 256)
        return pl.ds(pl.multiple_of(start, 128), 256)

    tcp = [copy(f96.at[hrows(c), window(zo(d))], fw.at[z], peer) for d, peer in zip(range(1, nz), line_z)]
    fw[z] = f96[hrows(c), window(z)]
    ncp = copy(f96.at[0:16, :], fn, dev(z_=zo(-1)))
    step(vocabulary)

    pump(heads)
    preact = dot(f96[hrows(c), :], hg[...].reshape(d_model, kcols))
    sigma = jax.nn.sigmoid(preact)
    gfac[...] = sigma * (1.0 + preact * (1.0 - sigma))
    student = f96[hrows(c), ycols(y)].astype(F32) + preact * sigma
    sg[c, x, :, ycols(y)] = student.astype(BF16)

    fwd = []
    part = lambda i, j, rows: sg.at[c, j, rows, ALL if i is ALL else ycols(i)]
    gather(part, y_ring, forward_to(fwd, same, partner), [nothing, lambda: step(vocabulary)])
    pump(vocabulary)
    ncp.wait_recv()
    voc = vg[...].reshape(d_model, vcols)
    n_st = NX * grp
    ls[n_st : n_st + grp, :] = dot(f96[...], voc)
    ls[n_st + grp : n_st + grp + 16, :] = dot(fn[...], voc)
    ls[n_st + grp + 16 :, :] = jnp.zeros((16, vcols), F32)
    arrive(fwd)
    ls[0:n_st, :] = dot(sg[...].reshape(n_st, d_model), voc)

    def reduce_plane(src, first_in, second_in, result):
        cps = [copy(src, first_in.at[x * 2 + c], peer) for peer in plane]
        yield
        arrive(cps)
        row = src[...]
        for a, b in near:
            row = row + first_in[a * 2 + b]
        second_in[y] = row
        cps = [same(second_in.at[y], peer) for peer in line_y]
        yield
        arrive(cps)
        row = second_in[0]
        for i in range(1, ny):
            row = row + second_in[i]
        result.append(row)

    ones = jnp.ones((8, vcols), F32)
    sums[...] = dot(ones, jnp.exp(ls[...]), ((1,), (1,)), HIGHEST)[0:1, :]
    result = []
    pump(reduce_plane(sums, r1, r2, result))
    logs = jnp.log(result[0])
    n_all = ls.shape[0]
    column = dot(jnp.broadcast_to(logs, (8, n_all)), first_row, ((0,), (0,)), HIGHEST)[:, 0:1]
    tl[...] = ls[n_st : n_st + tl.shape[0], :] - column[n_st : n_st + tl.shape[0]]
    losses = [None] * NX
    row_id = iota((ROWS, 1), 0)
    n_tok = nz * grp
    for h in range(2):
        for k in range(NX):
            at = (h * NX + k) * ROWS
            logp = ls[at : at + ROWS, :] - column[at : at + ROWS]
            target = tl[h * ROWS + k + 1 : h * ROWS + k + 1 + ROWS, :]
            p = jnp.exp(target)
            weight = jnp.where(z * grp + h * ROWS + row_id + (k + 1) < n_tok, 1.0 / (n_tok - k - 1), 0.0)
            terms = jnp.sum(weight * (p * (target - logp)), axis=0, keepdims=True)
            losses[k] = terms if losses[k] is None else losses[k] + terms
            sl[h, k * ROWS : (k + 1) * ROWS, :] = (weight * (jnp.exp(logp) - p)).astype(BF16)
    for k in range(NX):
        lsum[:, k * 128 : (k + 1) * 128] = losses[k][:, :128] + losses[k][:, 128:]

    def fill_back(dst, core, o):
        value = dot(sl[core], vg[yo(o)], ((1,), (1,)))
        dst[yo(o)] = value.astype(dst.dtype).reshape(NX, ROWS, kcols)

    loss_rows = []

    def loss_task():
        result = []
        yield from reduce_plane(lsum, q1, q2, result)
        q3[z] = result[0]
        cps = [same(q3.at[z], peer) for peer in line_z]
        yield
        arrive(cps)
        row = q3[0]
        for i in range(1, nz):
            row = row + q3[i]
        loss_rows.append(row)

    def turn():
        arrive(tcp)
        lhs_t[...] = fw[...].reshape(nz * ROWS, 256).astype(F32).T.astype(BF16)

    task = loss_task()
    go_on = lambda: step(task)
    go_on()
    back = scatter(fill_back, y_ring, hset, [go_on, go_on])
    gg[z, x] = (back * gfac[...]).astype(BF16)

    gather(lambda i, j, rows: gg.at[i, j, rows], z_ring, None, [lambda: (turn(), go_on())])

    cut = dp * vrow - jnp.minimum(lax.div(dp * vrow, 128) * 128, d_model - 256)
    lhs = lhs_t[pl.ds(pl.multiple_of(cut, 32), vrow), :]
    cols = kcols // 2
    for k in range(NX):
        o = dot(lhs, gg[:, k].reshape(nz * ROWS, kcols))
        low, high = o[:, :cols], o[:, cols:]
        osd[k] = jnp.where(c == 0, high, low).astype(BF16)
        out_ref[k] = jnp.where(c == 0, low, high)
    ocp = copy(osd, ord_, partner)
    row = loss_rows[0]
    for k in range(NX):
        loss_ref[k] = jnp.sum(row[:, k * 128 : (k + 1) * 128])
    ocp.wait_recv()
    out_ref[...] = out_ref[...] + ord_[...].astype(F32)
    for cp in sent:
        cp.wait_send()


def forward_to(forwards, same, partner):
    return lambda ref: forwards.append(same(ref, partner))


def solution(mesh):
    nz, ny = mesh.shape["dp"] // NX, mesh.shape["expert"] // 2

    def shards(tokens, routes, w_router, norm_gain, w_gate, w_up, w_down, final_gain, head_weights, vocab_proj):
        d_model = tokens.shape[1]
        half = d_model // 2
        kcols = d_model // ny
        vcols = vocab_proj.shape[1] // NX
        grp = NX * TOK
        vm = pltpu.VMEM

        def scatter_set(n, own):
            return (
                vm((n, NX, ROWS, kcols), own),
                vm((n, NX, ROWS, kcols), BF16),
                vm((n, NX, ROWS, kcols), BF16),
                vm((NX - 1, n, ROWS, kcols), BF16),
                vm((NX - 1, n, ROWS, kcols), BF16),
                vm((n, ROWS, kcols), BF16),
                vm((n, ROWS, kcols), BF16),
            )

        flat = [
            vm(tokens.shape, BF16),
            vm(routes.shape[::-1], jnp.int32),
            vm(w_router.shape[::-1], BF16),
            vm((1, d_model), F32),
            vm((1, d_model), F32),
            vm(head_weights.shape, BF16),
            vm((d_model, 256), BF16),
            vm((2, 128, half), BF16),
            vm((nz, d_model // nz, vcols), BF16),
            vm((NX, ROWS, kcols // 2), BF16),
            vm((NX, ROWS, kcols), BF16),
            vm((nz, NX, 2, ROWS, kcols), BF16),
            vm((2, NX, TOK, half), BF16),
            vm((2 * NX, grp, kcols), F32),
            vm((2 * NX, grp, kcols), BF16),
            vm((2, nz, NX, ROWS, kcols), BF16),
            vm((ny, ROWS, kcols), BF16),
            vm((2, NX, grp, kcols), BF16),
            vm((grp, d_model), BF16),
            vm((nz, ROWS, 256), BF16),
            vm((16, d_model), BF16),
            vm((ROWS, kcols), F32),
            vm((2, NX, ROWS, d_model), BF16),
            vm((512, vcols), F32),
            vm((grp + 16, vcols), F32),
            vm((1, 512), F32),
            vm((1, 512), F32),
            vm((2, NX * ROWS, vcols), BF16),
            vm((nz, NX, ROWS, kcols), BF16),
            vm((NX, 96, kcols // 2), BF16),
            vm((NX, 96, kcols // 2), BF16),
            vm((256, nz * ROWS), BF16),
            vm((1, 128), F32),
            vm((2 * NX, 1, 128), F32),
            vm((2 * NX, 1, 512), F32),
            vm((ny, 1, 512), F32),
            vm((2 * NX, 1, 512), F32),
            vm((ny, 1, 512), F32),
            vm((nz, 1, 512), F32),
        ]
        scratch = flat + [
            scatter_set(nz, F32),
            scatter_set(ny, F32),
            pltpu.SemaphoreType.DMA((N_COPIES,)),
            pltpu.SemaphoreType.DMA((N_COPIES,)),
            pltpu.SemaphoreType.DMA((16,)),
        ]

        def kernel(*refs):
            body(nz, ny, *refs)

        in_vmem = pl.BlockSpec(memory_space=pltpu.VMEM)
        in_hbm = pl.BlockSpec(memory_space=pl.ANY)
        losses, grads = pl.pallas_call(
            kernel,
            out_shape=(
                jax.ShapeDtypeStruct((NX,), F32),
                jax.ShapeDtypeStruct((NX, 96, kcols // 2), F32),
            ),
            in_specs=[in_hbm] * 10,
            out_specs=(pl.BlockSpec(memory_space=pltpu.SMEM), in_vmem),
            scratch_shapes=scratch,
            compiler_params=pltpu.CompilerParams(
                collective_id=0, has_side_effects=True, vmem_limit_bytes=60 * 2**20
            ),
            name="step",
        )(
            tokens,
            routes.T,
            w_router.T,
            norm_gain[None],
            final_gain[None],
            head_weights,
            w_gate[0],
            w_up[0],
            w_down[0],
            vocab_proj,
        )
        return losses, grads

    in_specs = (
        P("dp", None),
        P(),
        P(),
        P(),
        P("expert", None, "dp"),
        P("expert", None, "dp"),
        P("expert", "dp", None),
        P(),
        P(None, "dp", "expert"),
        P("dp", "expert"),
    )
    out_specs = (P(), P(None, "dp", "expert"))
    return jax.shard_map(shards, mesh=mesh, in_specs=in_specs, out_specs=out_specs, check_vma=False)
```
